32 devices in a mesh: tm: 8 (over z, x), state: 4 (over y, core).
Axes of the slice: x: 2, y: 2, z: 4, core: 2. Of those that a mesh axis runs over, the one named last changes fastest.
Arguments:
- trans_weight: bfloat16 [8, 2048, 2048], P('tm', None, 'state'), may hold values from 6e-06 to 163000
- pattern: int32 [16, 16], replicated, may hold values 0 or 1
- boundary: int32 [8], P('tm'), may hold values 0 or 1
- log_emit: float32 [8, 2048], P('tm', 'state'), may hold values from -63 to 153
Outputs:
- quad_op: float32 [4096, 2048], P('tm', 'state')
The draws below stay inside these ranges and needn't reach their ends.
All inputs are finite; a program needn't handle non-finite values. No bound on the sum of `boundary` on one device may be relied on, other than what follows from the above.
Results may differ from the reference program's by a relative error of at most 0.0003.
Values sent between devices are 32-bit elements; how exact they have to be, the bound alone decides.
A program may use at most 64 MiB of HBM per device.

```python
import jax
import jax.numpy as jnp
from jax import lax

S = 2048
BLOCK = 128
NBLK = 16
TIME = 8
QUADS = 2


def draw_log_emit(key, part):
    key_noise = jax.random.fold_in(key, 1)
    return jnp.clip(1.5 * jax.random.normal(key_noise, (TIME, S), jnp.float32), -9.0, 9.0)


def draw_trans_weight(key, part):
    key_weight = jax.random.fold_in(key, 17)
    spread = 3.0 * jnp.clip(jax.random.normal(key_weight, (TIME, S, S), jnp.float32), -4.0, 4.0)
    return jnp.exp(spread).astype(jnp.bfloat16)


def place_ends(entries, key, smallest, largest):
    longest = entries.shape.index(max(entries.shape))
    spots = []
    for shift in (0, 1):
        where = [jax.random.randint(jax.random.fold_in(key, axis), (), 0, length) for axis, length in enumerate(entries.shape)]
        where[longest] = (where[longest] + shift) % entries.shape[longest]
        spots.append(tuple(where))
    return entries.at[spots[0]].set(smallest).at[spots[1]].set(largest)


def setup_inputs(seed: int = 0) -> dict:
    splits = jax.random.split(jax.random.key(seed), 5)
    return {
        "trans_weight": draw_trans_weight(jax.random.fold_in(splits[4], 71), 0),
        "pattern": place_ends((jax.random.randint(splits[1], (NBLK, NBLK), 0, 8) < 3).astype(jnp.int32), jax.random.fold_in(splits[1], 1), 0, 1),
        "boundary": place_ends((jax.random.randint(splits[2], (TIME,), 0, 4) < 1).astype(jnp.int32), jax.random.fold_in(splits[2], 1), 0, 1),
        "log_emit": draw_log_emit(jax.random.fold_in(splits[4], 71), 0),
    }


def step_op(weight, pattern, marker, emission):
    states = weight.shape[0]
    blocks = jnp.arange(states, dtype=jnp.int32) // BLOCK
    block_mask = pattern[blocks][:, blocks].astype(jnp.float32)
    restart = 0.0001 + 0.4999 * marker.astype(jnp.float32)
    mixture = (1.0 - restart) * (4.0 / states) * weight.astype(jnp.float32) * block_mask + restart / states
    return jnp.log(mixture) + emission[None, :]


def combine(left_log, right_log):
    row_top = jnp.max(left_log, axis=1, keepdims=True)
    col_top = jnp.max(right_log, axis=0, keepdims=True)
    lead = lax.optimization_barrier(jnp.exp(left_log - row_top).astype(jnp.bfloat16)).astype(jnp.float32)
    trail = lax.optimization_barrier(jnp.exp(right_log - col_top).astype(jnp.bfloat16)).astype(jnp.float32)
    summed = jnp.dot(lead, trail, precision=lax.Precision.HIGHEST)
    return row_top + col_top + jnp.log(summed)


def reference(trans_weight, pattern, boundary, log_emit):
    def one_quad(quad_index):
        operators = []
        for member in range(4):
            position = quad_index * 4 + member
            weight = lax.dynamic_index_in_dim(trans_weight, position, 0, False)
            marker = lax.dynamic_index_in_dim(boundary, position, 0, False)
            emission = lax.dynamic_index_in_dim(log_emit, position, 0, False)
            operators.append(step_op(weight, pattern, marker, emission))
        first_pair = combine(operators[0], operators[1])
        second_pair = combine(operators[2], operators[3])
        return combine(first_pair, second_pair)

    stacked = lax.map(one_quad, jnp.arange(QUADS, dtype=jnp.int32))
    return stacked.reshape(QUADS * S, S)
```

```python
import functools
import math

import jax
import jax.numpy as jnp
from jax import lax
from jax.experimental import pallas as pl
from jax.experimental.pallas import tpu as pltpu
from jax.sharding import PartitionSpec as P

BLOCK = 128
ROWS = 64
FINE = 32
RELAY = 3
HAVE = 4
NEAR_RELAY = 3
NEAR_HAVE = 4
NEAR_LATER = 8
STRIPS = 4
PIECES = 2
SCHEDULE = (
    (0, 16, ((0, 0), (0, 1)), ()), (16, 19, (), ((0, 0), (0, 1))), (19, 21, ((1, 0), (1, 1)), ()),
    (21, 24, (), ((1, 0), (1, 1))), (24, 26, ((2, 0), (2, 1)), ()), (26, 29, (), ((2, 0), (2, 1))),
    (29, 30, ((3, 0),), ()), (30, 31, ((3, 1),), ()), (31, 32, (), ((3, 0), (3, 1))),
)
LEAD_SHIFT = 12
TRAIL_SHIFT = -49
MESH = pl.DeviceIdType.MESH


def kernel(
    parts, w_hbm, pattern_ref, boundary_ref, emit_ref, out_ref,
    w_ref, aux_ref, left, trail, pair, paired, first, stage, right, infos,
    load, info_send, info_recv, x_send, x_recv, y_send, y_recv, c_recv, p_send, p_recv,
    q_send, q_recv, g_send, g_recv, k_recv, b_send, b_recv, w_send, w_recv, v_send, v_recv,
):
    states, width = w_ref.shape
    blocks = states // BLOCK
    chunks = states // ROWS
    fine = states // FINE
    per_quarter = chunks // 4
    half = chunks // 2
    half_states = states // 2
    quarter_rows = states // 4
    strip = width // STRIPS
    piece = quarter_rows // PIECES
    tm = lax.axis_index("tm")
    s = lax.axis_index("state")
    base = tm // 4 * 4
    member = tm % 4
    p = member // 2
    h = member % 2
    me = member * parts + s
    core = s + 1 - 2 * (s % 2)
    over = (s + 2) % 4
    total = 4 * parts

    def device(p_, h_, s_):
        return (base + 2 * p_ + h_, s_)

    barrier = pltpu.get_barrier_semaphore()
    for k in range(1, total):
        peer = (me + k) % total
        pl.semaphore_signal(barrier, inc=1, device_id=(base + peer // parts, peer % parts), device_id_type=MESH)

    loading = pltpu.make_async_copy(w_hbm, w_ref, load.at[0])
    loading.start()

    restart = 0.0001 + 0.4999 * jnp.full((1, width), boundary_ref[0]).astype(jnp.float32)
    column = lax.broadcasted_iota(jnp.int32, (blocks, width), 1) // BLOCK + s * (width // BLOCK)
    chosen = (column == lax.broadcasted_iota(jnp.int32, (blocks, width), 0)).astype(jnp.float32)
    mine = jnp.dot(pattern_ref[...].astype(jnp.float32), chosen, preferred_element_type=jnp.float32)
    aux_ref[0:blocks, :] = mine * (4.0 * (1.0 - restart) / restart)
    aux_ref[blocks:blocks + 1, :] = emit_ref[...]
    aux_ref[blocks + 1:blocks + 8, :] = jnp.broadcast_to(jnp.log(restart / states), (7, width))

    pl.semaphore_wait(barrier, total - 1)

    info = aux_ref.at[pl.ds(blocks, 8)]

    def info_copy(k):
        peer = (me + k) % total
        return pltpu.make_async_remote_copy(
            src_ref=info, dst_ref=infos.at[me], send_sem=info_send.at[0], recv_sem=info_recv.at[k],
            device_id=(base + peer // parts, peer % parts), device_id_type=MESH)

    for k in range(1, total):
        info_copy(k).start()
    infos[me] = aux_ref[blocks:blocks + 8, :]
    loading.wait()

    def remote(src, dst, send, recv, target):
        return pltpu.make_async_remote_copy(
            src_ref=src, dst_ref=dst, send_sem=send, recv_sem=recv, device_id=target, device_id_type=MESH)

    def same(view, send, recv, target):
        return remote(view, view, send, recv, target)

    def fine_row(i):
        return pl.multiple_of(i * FINE, FINE)

    def local_row(g):
        return pl.multiple_of(g * ROWS, ROWS)

    def half_rows(i, side):
        return pl.multiple_of(((2 + side - 2 * (i % 2)) * per_quarter + i // 2) * ROWS, ROWS)

    def columns(n):
        return pl.ds(n * strip, strip)

    def piece_rows(j):
        return pl.ds(j * piece, piece)

    def x_copy(i, row, count):
        return same(left.at[s, pl.ds(row, count)], x_send.at[0], x_recv.at[i], device(p, 1 - h, s))

    def y_over(i, row, count, slot):
        return same(left.at[slot, pl.ds(row, count)], y_send.at[1], y_recv.at[i], device(p, h, over))

    def y_core(kind, i, row, count, slot):
        return same(left.at[slot, pl.ds(row, count)], y_send.at[kind], c_recv.at[i], device(p, h, core))

    def pair_copy(kind, i, target):
        return same(pair.at[pl.ds(fine_row(i), FINE)], p_send.at[kind], p_recv.at[i], target)

    def g_over(g, slot):
        return same(first.at[slot, pl.ds(local_row(g), ROWS)], g_send.at[1], g_recv.at[g], device(p, h, over))

    def g_core(kind, g, slot):
        return same(first.at[slot, pl.ds(local_row(g), ROWS)], g_send.at[kind], k_recv.at[0], device(p, h, core))

    def strip_over(n, j, slot):
        view = first.at[slot, piece_rows(j), columns(n)]
        return same(view, g_send.at[1], g_recv.at[n * PIECES + j], device(p, h, over))

    def strip_core(kind, n, j, slot):
        return same(first.at[slot, piece_rows(j), columns(n)], g_send.at[kind], k_recv.at[0], device(p, h, core))

    def q_copy(g):
        rows = pl.ds(local_row(g), ROWS)
        return remote(stage.at[rows], first.at[s, rows], q_send.at[0], q_recv.at[g], device(1 - p, 1, s))

    def q_piece(n, j):
        return remote(
            stage.at[piece_rows(j), columns(n)], first.at[s, piece_rows(j), columns(n)],
            q_send.at[0], q_recv.at[n * PIECES + j], device(1 - p, 0, s))

    def w_copy(g):
        return remote(
            stage.at[pl.ds(local_row(g), ROWS)], stage.at[pl.ds(local_row(g + per_quarter), ROWS)],
            w_send.at[0], w_recv.at[g], device(p, h, over))

    def v_copy(g):
        return remote(
            stage.at[pl.ds(local_row(g + per_quarter), ROWS)], first.at[over, pl.ds(local_row(g), ROWS)],
            v_send.at[0], v_recv.at[g], device(1 - p, 1, s))

    def b_copy(n):
        return same(right.at[:, columns(n)], b_send.at[0], b_recv.at[n], device(p, 1 - h, s))

    def odds(row, count):
        gain = aux_ref[pl.ds(row // BLOCK, 1), :]
        return 1.0 + w_ref[pl.ds(row, count), :].astype(jnp.float32) * gain

    def loop(count, body):
        def run(i, c):
            body(i)
            return c
        lax.fori_loop(0, count, run, 0)

    @pl.when((h == 0) & (p == 1))
    def _():
        @functools.partial(loop, fine)
        def _(i):
            row = fine_row(i)
            left[s, pl.ds(row, FINE), :] = odds(row, FINE)
            x_copy(i, row, FINE).start()

    @pl.when((h == 0) & (p == 0))
    def _():
        @functools.partial(loop, half)
        def _(i):
            row = half_rows(i, 1)
            left[s, pl.ds(row, ROWS), :] = odds(row, ROWS)
            x_copy(i, row, ROWS).start()
            near = half_rows(i, 0)
            left[s, pl.ds(near, ROWS), :] = odds(near, ROWS)
            y_over(i, near, ROWS, s).start()
            y_core(0, i, near, ROWS, s).start()

    @pl.when((h == 1) & (p == 1))
    def _():
        @functools.partial(loop, chunks)
        def _(i):
            row = local_row(i)
            trail[pl.ds(row, ROWS), :] = odds(row, ROWS).astype(jnp.bfloat16)

    @pl.when((h == 1) & (p == 0))
    def _():
        for n in range(STRIPS):
            @functools.partial(loop, chunks)
            def _(i):
                row = local_row(i)
                gain = aux_ref[pl.ds(row // BLOCK, 1), :][:, n * strip:(n + 1) * strip]
                value = 1.0 + w_ref[pl.ds(row, ROWS), columns(n)].astype(jnp.float32) * gain
                right[pl.ds(row, ROWS), columns(n)] = value
                trail[pl.ds(row, ROWS), columns(n)] = value.astype(jnp.bfloat16)
            b_copy(n).start()

    for k in range(1, total):
        sender = (me + total - k) % total
        pltpu.make_async_remote_copy(
            src_ref=info, dst_ref=infos.at[sender], send_sem=info_send.at[0], recv_sem=info_recv.at[k],
            device_id=(base + sender // parts, sender % parts), device_id_type=MESH).wait_recv()

    def emission(m, part):
        return infos[m * parts + part, 0:1, :]

    def peak(m):
        top = emission(m, 0)
        for part in range(1, parts):
            top = jnp.maximum(top, emission(m, part))
        return jnp.max(top, axis=1, keepdims=True)

    left_peak = jnp.where(p == 0, peak(0), peak(2))
    weights = [
        jnp.exp(jnp.where(p == 0, emission(0, part), emission(2, part)) - left_peak) for part in range(parts)
    ]
    middle_peak = peak(1)
    middle_emission = infos[parts + s, 0:1, :]
    middle_scale = jnp.exp(middle_emission - middle_peak) * 2.0 ** LEAD_SHIFT

    def product(row, count, n):
        acc = None
        for part in range(parts):
            lead = (left[part, pl.ds(row, count), :] * weights[part]).astype(jnp.bfloat16)
            block = slice(part * width, (part + 1) * width)
            right_block = trail[block, :] if n is None else trail[block, n * strip:(n + 1) * strip]
            term = jnp.dot(lead, right_block, preferred_element_type=jnp.float32)
            acc = term if acc is None else acc + term
        return acc

    def take(i, row, count):
        x_copy(i, row, count).wait_recv()
        y_over(i, row, count, s).start()
        y_core(0, i, row, count, s).start()

    def relay(i, row, count):
        y_over(i, row, count, over).wait_recv()
        y_core(2, i, row, count, over).start()

    def have(i, row, count):
        view = left.at[pl.ds(0, 2), pl.ds(row, count)]
        same(view, y_send.at[0], c_recv.at[i], device(p, h, core)).wait_recv()

    @pl.when((p == 1) & (h == 1))
    def _():
        @functools.partial(loop, fine + HAVE)
        def _(t):
            @pl.when(t < fine)
            def _():
                take(t, fine_row(t), FINE)

            @pl.when((t >= RELAY) & (t < fine + RELAY))
            def _():
                relay(t - RELAY, fine_row(t - RELAY), FINE)

            @pl.when(t >= HAVE)
            def _():
                i = t - HAVE
                row = fine_row(i)
                have(i, row, FINE)
                value = product(row, FINE, None) * 2.0 ** TRAIL_SHIFT
                pair[pl.ds(row, FINE), :] = value
                pair_copy(0, i, device(0, 1, s)).start()
                pair_copy(1, i, device(1, 0, s)).start()
                paired[pl.ds(row, FINE), :] = value.astype(jnp.bfloat16)

        @functools.partial(loop, per_quarter)
        def _(g):
            q_copy(g).wait_recv()
            g_core(0, g, s).start()
            v_copy(g).wait_recv()
            g_core(2, g, over).start()

    @pl.when((p == 0) & (h == 1))
    def _():
        @functools.partial(loop, half + NEAR_LATER)
        def _(t):
            @pl.when(t < half)
            def _():
                take(t, half_rows(t, 1), ROWS)

            @pl.when((t >= NEAR_RELAY) & (t < half + NEAR_RELAY))
            def _():
                relay(t - NEAR_RELAY, half_rows(t - NEAR_RELAY, 1), ROWS)

            @pl.when((t >= NEAR_HAVE) & (t < half + NEAR_HAVE))
            def _():
                i = t - NEAR_HAVE
                g = i // 2
                row = half_rows(i, 1)
                have(i, row, ROWS)
                value = product(row, ROWS, None) * middle_scale

                @pl.when(i % 2 == 0)
                def _():
                    stage[pl.ds(local_row(g), ROWS), :] = value
                    w_copy(g).start()
                    q_copy(g).start()

                @pl.when(i % 2 == 1)
                def _():
                    first[s, pl.ds(local_row(g), ROWS), :] = value
                    g_over(g, s).start()
                    g_core(0, g, s).start()

            @pl.when(t >= NEAR_LATER)
            def _():
                i = t - NEAR_LATER
                g = i // 2

                @pl.when(i % 2 == 0)
                def _():
                    w_copy(g).wait_recv()
                    v_copy(g).start()

                @pl.when(i % 2 == 1)
                def _():
                    g_over(g, over).wait_recv()
                    g_core(2, g, over).start()

    def strip_out(n, j):
        strip_over(n, j, s).start()
        strip_core(0, n, j, s).start()

    def strip_relay(n, j):
        strip_over(n, j, over).wait_recv()
        strip_core(2, n, j, over).start()

    def arrive(i):
        pair_copy(0, i, device(0, h, s)).wait_recv()

    def round_pair(i):
        row = fine_row(i)
        paired[pl.ds(row, FINE), :] = pair[pl.ds(row, FINE), :].astype(jnp.bfloat16)

    @pl.when((p == 1) & (h == 0))
    def _():
        for low, high, arrivals, passes in SCHEDULE:
            def relay_pair(i, c):
                arrive(i)
                pair_copy(0, i, device(0, 0, s)).start()
                round_pair(i)
                return c
            lax.fori_loop(fine * low // 32, fine * high // 32, relay_pair, 0)
            for n, j in arrivals:
                q_piece(n, j).wait_recv()
                strip_out(n, j)
            for n, j in passes:
                strip_relay(n, j)

    @pl.when((p == 0) & (h == 0))
    def _():
        @functools.partial(loop, half)
        def _(i):
            relay(i, half_rows(i, 0), ROWS)

        @functools.partial(loop, half)
        def _(i):
            have(i, half_rows(i, 0), ROWS)

        for n in range(STRIPS):
            b_copy(n).wait_recv()

            @functools.partial(loop, chunks)
            def _(i):
                row = local_row(i)
                trail[pl.ds(row, ROWS), columns(n)] = right[pl.ds(row, ROWS), columns(n)].astype(jnp.bfloat16)

            scale = middle_scale[:, n * strip:(n + 1) * strip]
            for j in range(PIECES):
                stage[piece_rows(j), columns(n)] = product(2 * quarter_rows + j * piece, piece, n) * scale
                q_piece(n, j).start()
            for j in range(PIECES):
                first[s, piece_rows(j), columns(n)] = product(j * piece, piece, n) * scale
                strip_out(n, j)
            if n > 0:
                for j in range(PIECES):
                    strip_relay(n - 1, j)
        for j in range(PIECES):
            strip_relay(STRIPS - 1, j)

    early = fine * 7 // 8

    def bring(low, high):
        def run(i, c):
            arrive(i)
            round_pair(i)
            return c
        lax.fori_loop(low, high, run, 0)

    @pl.when(p == 0)
    def _():
        bring(0, early)

    same(first.at[pl.ds(0, 2)], g_send.at[0], k_recv.at[0], device(p, h, core)).wait_recv()

    log_shares = infos[0, 1:2, :] + infos[parts, 1:2, :] + infos[2 * parts, 1:2, :] + infos[3 * parts, 1:2, :]
    shift = math.log(2.0) * (LEAD_SHIFT + TRAIL_SHIFT)
    last_emission = jnp.zeros_like(middle_emission)
    for part in range(parts):
        last_emission = jnp.where(s == part, emission(3, part), last_emission)
    offset = last_emission + log_shares + (peak(0) + middle_peak + peak(2) - shift)

    tile = 256

    def partial_sum(row, low, high):
        acc = None
        for part in range(parts):
            begin, end = max(low, part * width), min(high, (part + 1) * width)
            if begin < end:
                lead = first[part, pl.ds(row, tile), begin - part * width:end - part * width].astype(jnp.bfloat16)
                term = jnp.dot(lead, paired[begin:end, :], preferred_element_type=jnp.float32)
                acc = term if acc is None else acc + term
        return acc

    cut = early * FINE

    @functools.partial(loop, quarter_rows // tile)
    def _(i):
        row = pl.multiple_of(i * tile, tile)
        out_ref[pl.ds(row, tile), :] = partial_sum(row, 0, cut)

    @pl.when(p == 0)
    def _():
        bring(early, fine)

    @functools.partial(loop, quarter_rows // tile)
    def _(i):
        row = pl.multiple_of(i * tile, tile)
        out_ref[pl.ds(row, tile), :] = jnp.log(out_ref[pl.ds(row, tile), :] + partial_sum(row, cut, states)) + offset

    same(infos.at[pl.ds(0, total - 1)], info_send.at[0], info_recv.at[0], device(p, h, core)).wait_send()

    def sent(view, sem):
        same(view, sem, load.at[0], device(p, h, core)).wait_send()

    def sent_left(count):
        for kind in range(3):
            sent(left.at[0, pl.ds(0, count)], y_send.at[kind])

    sent(first.at[0], g_send.at[0])
    sent(first.at[0], g_send.at[2])

    @pl.when((p == 0) | (h == 0))
    def _():
        sent(first.at[0], g_send.at[1])

    @pl.when((p == 1) & (h == 1))
    def _():
        sent_left(states)
        sent(pair, p_send.at[0])
        sent(pair, p_send.at[1])

    @pl.when((p == 1) & (h == 0))
    def _():
        sent(left.at[0], x_send.at[0])
        sent(pair, p_send.at[0])

    @pl.when((p == 0) & (h == 1))
    def _():
        sent(right, b_send.at[0])
        sent_left(half_states)
        sent(stage.at[pl.ds(0, quarter_rows)], q_send.at[0])
        sent(stage.at[pl.ds(0, quarter_rows)], w_send.at[0])
        sent(stage.at[pl.ds(0, quarter_rows)], v_send.at[0])

    @pl.when((p == 0) & (h == 0))
    def _():
        sent(left.at[0, pl.ds(0, half_states)], x_send.at[0])
        sent_left(half_states)
        sent(stage.at[pl.ds(0, quarter_rows)], q_send.at[0])


def on_device(parts, trans_weight, pattern, boundary, log_emit):
    weight = trans_weight[0]
    states, width = weight.shape
    blocks = pattern.shape[0]
    fine = states // FINE
    pieces = states // ROWS // 4
    dma = pltpu.SemaphoreType.DMA
    vmem = pl.BlockSpec(memory_space=pltpu.VMEM)
    return pl.pallas_call(
        functools.partial(kernel, parts),
        out_shape=jax.ShapeDtypeStruct((states // 4, width), jnp.float32),
        in_specs=[pl.BlockSpec(memory_space=pl.ANY), vmem, pl.BlockSpec(memory_space=pltpu.SMEM), vmem],
        out_specs=vmem,
        scratch_shapes=[
            pltpu.VMEM((states, width), jnp.bfloat16),
            pltpu.VMEM((blocks + 8, width), jnp.float32),
            pltpu.VMEM((parts, states, width), jnp.float32),
            pltpu.VMEM((states, width), jnp.bfloat16),
            pltpu.VMEM((states, width), jnp.float32),
            pltpu.VMEM((states, width), jnp.bfloat16),
            pltpu.VMEM((parts, states // 4, width), jnp.float32),
            pltpu.VMEM((states // 2, width), jnp.float32),
            pltpu.VMEM((states, width), jnp.float32),
            pltpu.VMEM((4 * parts, 8, width), jnp.float32),
            dma((1,)), dma((1,)), dma((4 * parts,)),
            dma((1,)), dma((fine,)),
            dma((3,)), dma((fine,)), dma((fine,)),
            dma((2,)), dma((fine,)),
            dma((1,)), dma((pieces,)),
            dma((3,)), dma((pieces,)), dma((1,)),
            dma((1,)), dma((STRIPS,)),
            dma((1,)), dma((pieces,)), dma((1,)), dma((pieces,)),
        ],
        compiler_params=pltpu.CompilerParams(
            collective_id=0, has_side_effects=True, vmem_limit_bytes=52 * 1024 * 1024
        ),
    )(weight, pattern, boundary, log_emit)


def solution(mesh):
    return jax.shard_map(
        functools.partial(on_device, mesh.shape["state"]),
        mesh=mesh,
        in_specs=(P("tm", None, "state"), P(), P("tm"), P("tm", "state")),
        out_specs=P("tm", "state"),
        check_vma=False,
    )
```

```python
import functools
import math

import jax
import jax.numpy as jnp
from jax import lax
from jax.experimental import pallas as pl
from jax.experimental.pallas import tpu as pltpu
from jax.sharding import PartitionSpec as P

BLOCK = 128
ROWS = 64
FINE = 32
RELAY = 2
HAVE = 3
NEAR_FIRST = 2
NEAR_RELAY = 3
NEAR_HAVE = 4
NEAR_LATER = 8
STRIPS = 4
PIECES = 2
DETOUR = 256
DETOURS = 3
SCHEDULE = (
    (0, 33, ((0, 0), (0, 1)), (), None), (33, 37, ((1, 0), (1, 1)), (), None), (37, 39, (), ((0, 0), (0, 1)), None),
    (39, 42, (), ((1, 0), (1, 1)), None), (42, 49, ((2, 0), (2, 1)), (), None), (49, 54, (), ((2, 0), (2, 1)), None),
    (54, 57, (), (), 0), (57, 58, ((3, 0),), (), 1), (58, 59, (), (), 2), (59, 60, (), (), 3), (60, 61, ((3, 1),), (), None),
    (61, 63, (), ((3, 0),), None), (63, 64, (), ((3, 1),), None),
)
EARLY = ((0, 3), (4, 7), (8, 11), (12, 14))
LATE = ((3, 4), (7, 8), (11, 12), (14, 16))
LEAD_SHIFT = 12
TRAIL_SHIFT = -49
MESH = pl.DeviceIdType.MESH


def kernel(
    parts, w_hbm, pattern_hbm, boundary_ref, emit_hbm, out_ref,
    w_ref, pattern_ref, emit_ref, aux_ref, info, left, trail, pair, paired, first, stage, right, infos,
    load, info_send, info_recv, x_send, x_recv, y_send, y_recv, c_recv, p_send, p_recv,
    q_send, q_recv, g_send, g_recv, k_recv, b_send, b_recv, w_send, w_recv, v_send, v_recv, d_send, d_recv,
):
    states, width = w_ref.shape
    blocks = states // BLOCK
    chunks = states // ROWS
    fine = states // FINE
    per_quarter = chunks // 4
    half = chunks // 2
    half_states = states // 2
    quarter_rows = states // 4
    strip = width // STRIPS
    piece = quarter_rows // PIECES
    tm = lax.axis_index("tm")
    s = lax.axis_index("state")
    base = tm // 4 * 4
    member = tm % 4
    p = member // 2
    h = member % 2
    me = member * parts + s
    core = s + 1 - 2 * (s % 2)
    over = (s + 2) % 4
    total = 4 * parts

    def device(p_, h_, s_):
        return (base + 2 * p_ + h_, s_)

    loads = [
        pltpu.make_async_copy(src, dst, load.at[k])
        for k, (src, dst) in enumerate(((pattern_hbm, pattern_ref), (emit_hbm, emit_ref), (w_hbm, w_ref)))
    ]
    for k in range(3):
        loads[k].start()

    barrier = pltpu.get_barrier_semaphore()
    for k in range(1, total):
        peer = (me + k) % total
        pl.semaphore_signal(barrier, inc=1, device_id=(base + peer // parts, peer % parts), device_id_type=MESH)

    for k in range(2):
        loads[k].wait()

    restart = 0.0001 + 0.4999 * jnp.full((1, width), boundary_ref[0]).astype(jnp.float32)
    column = lax.broadcasted_iota(jnp.int32, (blocks, width), 1) // BLOCK + s * (width // BLOCK)
    chosen = (column == lax.broadcasted_iota(jnp.int32, (blocks, width), 0)).astype(jnp.float32)
    mine = jnp.dot(pattern_ref[...].astype(jnp.float32), chosen, preferred_element_type=jnp.float32)
    aux_ref[...] = mine * (4.0 * (1.0 - restart) / restart)
    info[:, 0:width] = emit_ref[...]
    info[:, width:width + BLOCK] = jnp.log(restart / states)[:, 0:BLOCK]

    pl.semaphore_wait(barrier, total - 1)

    def info_copy(k):
        peer = (me + k) % total
        return pltpu.make_async_remote_copy(
            src_ref=info, dst_ref=infos.at[me], send_sem=info_send.at[0], recv_sem=info_recv.at[k],
            device_id=(base + peer // parts, peer % parts), device_id_type=MESH)

    loads[2].wait()
    infos[me] = info[...]

    def remote(src, dst, send, recv, target):
        return pltpu.make_async_remote_copy(
            src_ref=src, dst_ref=dst, send_sem=send, recv_sem=recv, device_id=target, device_id_type=MESH)

    def same(view, send, recv, target):
        return remote(view, view, send, recv, target)

    def fine_row(i):
        return pl.multiple_of(i * FINE, FINE)

    def local_row(g):
        return pl.multiple_of(g * ROWS, ROWS)

    def half_rows(i, side):
        return pl.multiple_of(((2 + side - 2 * (i // per_quarter)) * per_quarter + i % per_quarter) * ROWS, ROWS)

    def columns(n):
        return pl.ds(n * strip, strip)

    def piece_rows(j):
        return pl.ds(j * piece, piece)

    def x_copy(i, row, count):
        return same(left.at[s, pl.ds(row, count)], x_send.at[0], x_recv.at[i], device(p, 1 - h, s))

    def y_over(i, row, count, slot):
        return same(left.at[slot, pl.ds(row, count)], y_send.at[1], y_recv.at[i], device(p, h, over))

    def y_core(kind, i, row, count, slot):
        return same(left.at[slot, pl.ds(row, count)], y_send.at[kind], c_recv.at[i], device(p, h, core))

    def pair_copy(kind, i, target):
        return same(pair.at[pl.ds(fine_row(i), FINE)], p_send.at[kind], p_recv.at[i], target)

    def g_over(g, slot):
        return same(first.at[slot, pl.ds(local_row(g), ROWS)], g_send.at[1], g_recv.at[g], device(p, h, over))

    def g_core(kind, g, slot):
        return same(first.at[slot, pl.ds(local_row(g), ROWS)], g_send.at[kind], k_recv.at[0], device(p, h, core))

    def strip_over(n, j, slot):
        view = first.at[slot, piece_rows(j), columns(n)]
        return same(view, g_send.at[1], g_recv.at[n * PIECES + j], device(p, h, over))

    def strip_core(kind, n, j, slot):
        view = first.at[slot, piece_rows(j), columns(n)]
        return same(view, g_send.at[kind], k_recv.at[n // (STRIPS - 1)], device(p, h, core))

    def q_copy(g):
        rows = pl.ds(local_row(g), ROWS)
        return remote(stage.at[rows], first.at[s, rows], q_send.at[0], q_recv.at[g], device(1 - p, 1, s))

    def q_piece(n, j):
        return remote(
            stage.at[piece_rows(j), columns(n)], first.at[s, piece_rows(j), columns(n)],
            q_send.at[0], q_recv.at[n * PIECES + j], device(1 - p, 0, s))

    def w_copy(g):
        return remote(
            stage.at[pl.ds(local_row(g), ROWS)], stage.at[pl.ds(local_row(g + per_quarter), ROWS)],
            w_send.at[0], w_recv.at[g], device(p, h, over))

    def v_copy(g):
        return remote(
            stage.at[pl.ds(local_row(g + per_quarter), ROWS)], first.at[over, pl.ds(local_row(g), ROWS)],
            v_send.at[0], v_recv.at[g], device(1 - p, 1, s))

    def b_copy(n):
        begin = DETOUR * DETOURS if n == STRIPS - 1 else 0
        view = right.at[pl.ds(begin, states - begin), columns(n)]
        return same(view, b_send.at[0], b_recv.at[n], device(p, 1 - h, s))

    def d_copy(k, target):
        view = right.at[pl.ds(k * DETOUR, DETOUR), columns(STRIPS - 1)]
        return same(view, d_send.at[0], d_recv.at[k], target)

    def odds(row, count):
        gain = aux_ref[pl.ds(row // BLOCK, 1), :]
        return 1.0 + w_ref[pl.ds(row, count), :].astype(jnp.float32) * gain

    def loop(count, body, start=0):
        def run(i, c):
            body(i)
            return c
        lax.fori_loop(start, count, run, 0)

    def send_fine(i):
        row = fine_row(i)
        left[s, pl.ds(row, FINE), :] = odds(row, FINE)
        x_copy(i, row, FINE).start()

    def send_half(i):
        row = half_rows(i, 1)
        left[s, pl.ds(row, ROWS), :] = odds(row, ROWS)
        x_copy(i, row, ROWS).start()
        near = half_rows(i, 0)
        left[s, pl.ds(near, ROWS), :] = odds(near, ROWS)
        y_over(i, near, ROWS, s).start()
        y_core(0, i, near, ROWS, s).start()

    @pl.when((h == 0) & (p == 1))
    def _():
        send_fine(0)

    for k in range(1, total):
        info_copy(k).start()

    @pl.when((h == 0) & (p == 1))
    def _():
        loop(fine, send_fine, start=1)

    @pl.when((h == 0) & (p == 0))
    def _():
        loop(half, send_half)

    @pl.when((h == 1) & (p == 1))
    def _():
        @functools.partial(loop, chunks)
        def _(i):
            row = local_row(i)
            trail[pl.ds(row, ROWS), :] = odds(row, ROWS).astype(jnp.bfloat16)

    @pl.when((h == 1) & (p == 0))
    def _():
        for n in (STRIPS - 1,) + tuple(range(STRIPS - 1)):
            @functools.partial(loop, chunks)
            def _(i):
                row = local_row(i)
                gain = aux_ref[pl.ds(row // BLOCK, 1), :][:, n * strip:(n + 1) * strip]
                value = 1.0 + w_ref[pl.ds(row, ROWS), columns(n)].astype(jnp.float32) * gain
                right[pl.ds(row, ROWS), columns(n)] = value
                trail[pl.ds(row, ROWS), columns(n)] = value.astype(jnp.bfloat16)
            if n == STRIPS - 1:
                for k in range(DETOURS):
                    d_copy(k, device(1, 0, s)).start()
            else:
                b_copy(n).start()
        b_copy(STRIPS - 1).start()

    def take(i, row, count):
        x_copy(i, row, count).wait_recv()
        y_over(i, row, count, s).start()
        y_core(0, i, row, count, s).start()

    def relay(i, row, count):
        y_over(i, row, count, over).wait_recv()
        y_core(2, i, row, count, over).start()

    def have(i, row, count):
        view = left.at[pl.ds(0, 2), pl.ds(row, count)]
        same(view, y_send.at[0], c_recv.at[i], device(p, h, core)).wait_recv()

    def stream(t):
        @pl.when(t < fine)
        def _():
            take(t, fine_row(t), FINE)

        @pl.when((t >= RELAY) & (t < fine + RELAY))
        def _():
            relay(t - RELAY, fine_row(t - RELAY), FINE)

    @pl.when((p == 1) & (h == 1))
    def _():
        loop(HAVE, stream)

    @pl.when((p == 1) & (h == 0))
    def _():
        for k in range(DETOURS):
            d_copy(k, device(0, 0, s)).wait_recv()
            d_copy(k, device(0, 0, s)).start()

    def near_stream(t):
        @pl.when(t < half)
        def _():
            take(t, half_rows(t, 1), ROWS)

        @pl.when((t >= NEAR_RELAY) & (t < half + NEAR_RELAY))
        def _():
            relay(t - NEAR_RELAY, half_rows(t - NEAR_RELAY, 1), ROWS)

    @pl.when((p == 0) & (h == 1))
    def _():
        loop(NEAR_FIRST, near_stream)

    @pl.when((p == 0) & (h == 0))
    def _():
        @functools.partial(loop, half)
        def _(i):
            relay(i, half_rows(i, 0), ROWS)

    for k in range(1, total):
        sender = (me + total - k) % total
        pltpu.make_async_remote_copy(
            src_ref=info, dst_ref=infos.at[sender], send_sem=info_send.at[0], recv_sem=info_recv.at[k],
            device_id=(base + sender // parts, sender % parts), device_id_type=MESH).wait_recv()

    def emission(m, part):
        return infos[m * parts + part, :, 0:width]

    def peak(m):
        top = emission(m, 0)
        for part in range(1, parts):
            top = jnp.maximum(top, emission(m, part))
        return jnp.max(top, axis=1, keepdims=True)

    left_peak = jnp.where(p == 0, peak(0), peak(2))
    weights = [
        jnp.exp(jnp.where(p == 0, emission(0, part), emission(2, part)) - left_peak) for part in range(parts)
    ]
    middle_peak = peak(1)
    middle_emission = infos[parts + s, :, 0:width]
    middle_scale = jnp.exp(middle_emission - middle_peak) * 2.0 ** LEAD_SHIFT

    def product(row, count, n):
        acc = None
        for part in range(parts):
            lead = (left[part, pl.ds(row, count), :] * weights[part]).astype(jnp.bfloat16)
            block = slice(part * width, (part + 1) * width)
            right_block = trail[block, :] if n is None else trail[block, n * strip:(n + 1) * strip]
            term = jnp.dot(lead, right_block, preferred_element_type=jnp.float32)
            acc = term if acc is None else acc + term
        return acc

    @pl.when((p == 1) & (h == 1))
    def _():
        @functools.partial(loop, fine + HAVE, start=HAVE)
        def _(t):
            stream(t)

            i = t - HAVE
            row = fine_row(i)
            have(i, row, FINE)
            value = product(row, FINE, None) * 2.0 ** TRAIL_SHIFT
            pair[pl.ds(row, FINE), :] = value

            @pl.when(i == fine - 1)
            def _():
                pair_copy(2, i, device(0, 0, s)).start()

            pair_copy(0, i, device(0, 1, s)).start()
            pair_copy(1, i, device(1, 0, s)).start()
            paired[pl.ds(row, FINE), :] = value.astype(jnp.bfloat16)

            @pl.when((t >= fine - per_quarter) & (t < fine))
            def _():
                g = t - (fine - per_quarter)
                q_copy(g).wait_recv()
                g_core(0, g, s).start()
                v_copy(g).wait_recv()
                g_core(2, g, over).start()

    @pl.when((p == 0) & (h == 1))
    def _():
        @functools.partial(loop, half + NEAR_LATER, start=NEAR_FIRST)
        def _(t):
            near_stream(t)

            @pl.when((t >= NEAR_HAVE) & (t < half + NEAR_HAVE))
            def _():
                i = t - NEAR_HAVE
                g = i % per_quarter
                row = half_rows(i, 1)
                have(i, row, ROWS)
                value = product(row, ROWS, None) * middle_scale

                @pl.when(i < per_quarter)
                def _():
                    stage[pl.ds(local_row(g), ROWS), :] = value
                    w_copy(g).start()
                    q_copy(g).start()

                @pl.when(i >= per_quarter)
                def _():
                    first[s, pl.ds(local_row(g), ROWS), :] = value
                    g_over(g, s).start()
                    g_core(0, g, s).start()

            @pl.when(t >= NEAR_LATER)
            def _():
                i = t - NEAR_LATER
                g = i % per_quarter

                @pl.when(i < per_quarter)
                def _():
                    w_copy(g).wait_recv()
                    v_copy(g).start()

                @pl.when(i >= per_quarter)
                def _():
                    g_over(g, over).wait_recv()
                    g_core(2, g, over).start()

    unit = states // 16
    tile = quarter_rows // 4

    def partial_sum(row, ranges):
        acc = None
        for low, high in ranges:
            part, begin = low * unit // width, low * unit % width
            lead = first[part, pl.ds(row, tile), begin:begin + (high - low) * unit].astype(jnp.bfloat16)
            term = jnp.dot(lead, paired[low * unit:high * unit, :], preferred_element_type=jnp.float32)
            acc = term if acc is None else acc + term
        return acc

    def early_sum(i):
        row = pl.multiple_of(i * tile, tile)
        out_ref[pl.ds(row, tile), :] = partial_sum(row, EARLY)

    def wait_core(low, high, k):
        view = first.at[pl.ds(0, 2), :, pl.ds(low, high - low)]
        same(view, g_send.at[0], k_recv.at[k], device(p, h, core)).wait_recv()

    def strip_out(n, j):
        strip_over(n, j, s).start()
        strip_core(0, n, j, s).start()

    def strip_relay(n, j):
        strip_over(n, j, over).wait_recv()
        strip_core(2, n, j, over).start()

    def arrive(i):
        pair_copy(0, i, device(0, h, s)).wait_recv()

    def round_pair(i):
        row = fine_row(i)
        paired[pl.ds(row, FINE), :] = pair[pl.ds(row, FINE), :].astype(jnp.bfloat16)

    @pl.when((p == 1) & (h == 0))
    def _():
        for low, high, arrivals, passes, part_row in SCHEDULE:
            def relay_pair(i, c):
                arrive(i)

                @pl.when(i < fine - 1)
                def _():
                    pair_copy(0, i, device(0, 0, s)).start()

                round_pair(i)
                return c
            lax.fori_loop(fine * low // 64, fine * high // 64, relay_pair, 0)
            for n, j in arrivals:
                q_piece(n, j).wait_recv()
                strip_out(n, j)
            for n, j in passes:
                strip_relay(n, j)
            if part_row == 0:
                wait_core(0, width - strip, 0)
            if part_row is not None:
                early_sum(part_row)

    @pl.when((p == 0) & (h == 0))
    def _():
        @functools.partial(loop, half)
        def _(i):
            have(i, half_rows(i, 0), ROWS)

        for n in range(STRIPS):
            b_copy(n).wait_recv()
            if n == STRIPS - 1:
                for k in range(DETOURS):
                    d_copy(k, device(1, 0, s)).wait_recv()

            @functools.partial(loop, chunks)
            def _(i):
                row = local_row(i)
                trail[pl.ds(row, ROWS), columns(n)] = right[pl.ds(row, ROWS), columns(n)].astype(jnp.bfloat16)

            scale = middle_scale[:, n * strip:(n + 1) * strip]
            for j in range(PIECES):
                stage[piece_rows(j), columns(n)] = product(2 * quarter_rows + j * piece, piece, n) * scale
                q_piece(n, j).start()
            for j in range(PIECES):
                first[s, piece_rows(j), columns(n)] = product(j * piece, piece, n) * scale
                strip_out(n, j)
            if n > 0:
                for j in range(PIECES):
                    strip_relay(n - 1, j)
        for j in range(PIECES):
            strip_relay(STRIPS - 1, j)

    early = fine * 7 // 8

    def bring(low, high):
        def run(i, c):
            arrive(i)
            round_pair(i)
            return c
        lax.fori_loop(low, high, run, 0)

    @pl.when(p == 0)
    def _():
        bring(0, early)

    @pl.when(h == 1)
    def _():
        wait_core(0, width, 0)
        loop(4, early_sum)

    @pl.when((h == 0) & (p == 0))
    def _():
        wait_core(0, width - strip, 0)
        loop(4, early_sum)

    log_shares = jnp.zeros((1, 1), jnp.float32)
    for m in range(4):
        log_shares += infos[m * parts, :, width:width + 1]
    shift = math.log(2.0) * (LEAD_SHIFT + TRAIL_SHIFT)
    last_emission = jnp.zeros_like(middle_emission)
    for part in range(parts):
        last_emission = jnp.where(s == part, emission(3, part), last_emission)
    offset = last_emission + log_shares + (peak(0) + middle_peak + peak(2) - shift)

    @pl.when(h == 0)
    def _():
        wait_core(width - strip, width, 1)

    @pl.when(p == 0)
    def _():
        bring(early, fine)

    @functools.partial(loop, 4)
    def _(i):
        row = pl.multiple_of(i * tile, tile)
        out_ref[pl.ds(row, tile), :] = jnp.log(out_ref[pl.ds(row, tile), :] + partial_sum(row, LATE)) + offset

    same(infos.at[pl.ds(0, total - 1)], info_send.at[0], info_recv.at[0], device(p, h, core)).wait_send()

    def sent(view, sem):
        same(view, sem, load.at[0], device(p, h, core)).wait_send()

    def sent_left(count):
        for kind in range(3):
            sent(left.at[0, pl.ds(0, count)], y_send.at[kind])

    sent(first.at[0], g_send.at[0])
    sent(first.at[0], g_send.at[2])

    @pl.when((p == 0) | (h == 0))
    def _():
        sent(first.at[0], g_send.at[1])

    @pl.when((p == 1) & (h == 1))
    def _():
        sent_left(states)
        sent(pair, p_send.at[0])
        sent(pair, p_send.at[1])
        sent(pair.at[pl.ds(0, FINE)], p_send.at[2])

    @pl.when((p == 1) & (h == 0))
    def _():
        sent(left.at[0], x_send.at[0])
        sent(pair.at[pl.ds(0, states - FINE)], p_send.at[0])
        sent(right.at[pl.ds(0, DETOUR * DETOURS), columns(0)], d_send.at[0])

    @pl.when((p == 0) & (h == 1))
    def _():
        sent(right.at[pl.ds(0, states - DETOUR * DETOURS // STRIPS)], b_send.at[0])
        sent(right.at[pl.ds(0, DETOUR * DETOURS), columns(0)], d_send.at[0])
        sent_left(half_states)
        sent(stage.at[pl.ds(0, quarter_rows)], q_send.at[0])
        sent(stage.at[pl.ds(0, quarter_rows)], w_send.at[0])
        sent(stage.at[pl.ds(0, quarter_rows)], v_send.at[0])

    @pl.when((p == 0) & (h == 0))
    def _():
        sent(left.at[0, pl.ds(0, half_states)], x_send.at[0])
        sent_left(half_states)
        sent(stage.at[pl.ds(0, quarter_rows)], q_send.at[0])


def on_device(parts, trans_weight, pattern, boundary, log_emit):
    weight = trans_weight[0]
    states, width = weight.shape
    blocks = pattern.shape[0]
    fine = states // FINE
    pieces = states // ROWS // 4
    dma = pltpu.SemaphoreType.DMA
    hbm = pl.BlockSpec(memory_space=pl.ANY)
    return pl.pallas_call(
        functools.partial(kernel, parts),
        out_shape=jax.ShapeDtypeStruct((states // 4, width), jnp.float32),
        in_specs=[hbm, hbm, pl.BlockSpec(memory_space=pltpu.SMEM), hbm],
        out_specs=pl.BlockSpec(memory_space=pltpu.VMEM),
        scratch_shapes=[
            pltpu.VMEM((states, width), jnp.bfloat16),
            pltpu.VMEM((blocks, blocks), jnp.int32),
            pltpu.VMEM((1, width), jnp.float32),
            pltpu.VMEM((blocks, width), jnp.float32),
            pltpu.VMEM((1, width + BLOCK), jnp.float32),
            pltpu.VMEM((parts, states, width), jnp.float32),
            pltpu.VMEM((states, width), jnp.bfloat16),
            pltpu.VMEM((states, width), jnp.float32),
            pltpu.VMEM((states, width), jnp.bfloat16),
            pltpu.VMEM((parts, states // 4, width), jnp.float32),
            pltpu.VMEM((states // 2, width), jnp.float32),
            pltpu.VMEM((states, width), jnp.float32),
            pltpu.VMEM((4 * parts, 1, width + BLOCK), jnp.float32),
            dma((3,)), dma((1,)), dma((4 * parts,)),
            dma((1,)), dma((fine,)),
            dma((3,)), dma((fine,)), dma((fine,)),
            dma((3,)), dma((fine,)),
            dma((1,)), dma((pieces,)),
            dma((3,)), dma((pieces,)), dma((2,)),
            dma((1,)), dma((STRIPS,)),
            dma((1,)), dma((pieces,)), dma((1,)), dma((pieces,)), dma((1,)), dma((DETOURS,)),
        ],
        compiler_params=pltpu.CompilerParams(
            collective_id=0, has_side_effects=True, vmem_limit_bytes=52 * 1024 * 1024
        ),
    )(weight, pattern, boundary, log_emit)


def solution(mesh):
    return jax.shard_map(
        functools.partial(on_device, mesh.shape["state"]),
        mesh=mesh,
        in_specs=(P("tm", None, "state"), P(), P("tm"), P("tm", "state")),
        out_specs=P("tm", "state"),
        check_vma=False,
    )
```

```python
import functools
import math

import jax
import jax.numpy as jnp
from jax import lax
from jax.experimental import pallas as pl
from jax.experimental.pallas import tpu as pltpu
from jax.sharding import PartitionSpec as P

BLOCK = 128
ROWS = 64
FINE = 32
RELAY = 2
HAVE = 3
NEAR_FIRST = 2
NEAR_RELAY = 3
NEAR_HAVE = 4
NEAR_LATER = 8
STRIPS = 4
PIECES = 4
DIRECT = 1
DETOUR = 256
DETOURS = 2
SCHEDULE = (
    (0, 33, 0, None, None), (33, 37, 1, None, None), (37, 39, None, 0, None), (39, 42, None, 1, None),
    (42, 48, 2, None, None), (48, 52, None, 2, None), (52, 53, None, None, 0), (53, 54, None, None, 1),
    (54, 55, None, None, 2), (55, 56, None, None, 3),
)
LAST_SCHEDULE = ((56, 0, None), (57, 1, None), (58, 2, None), (59, 3, 0), (60, None, 1), (61, None, 2), (62, None, 3))
EARLY = ((0, 3), (4, 7), (8, 11))
MIDDLE = ((3, 4), (7, 8), (11, 12), (12, 15))
FINAL = ((15, 16),)
LEAD_SHIFT = 12
TRAIL_SHIFT = -49
MESH = pl.DeviceIdType.MESH


def kernel(
    parts, w_hbm, pattern_hbm, boundary_ref, emit_hbm, out_hbm, offset_ref,
    out_ref,    w_ref, pattern_ref, emit_ref, aux_ref, info, left, trail, pair, paired, first, stage, right, infos,
    load, info_send, info_recv, x_send, x_recv, y_send, y_recv, c_recv, p_send, p_recv,
    q_send, g_send, k_recv, b_send, b_recv, w_send, w_recv, v_send, v_recv, d_send, d_recv, o_send,
):
    states, width = w_ref.shape
    blocks = states // BLOCK
    chunks = states // ROWS
    fine = states // FINE
    per_quarter = chunks // 4
    half = chunks // 2
    half_states = states // 2
    quarter_rows = states // 4
    strip = width // STRIPS
    piece = quarter_rows // PIECES
    tm = lax.axis_index("tm")
    s = lax.axis_index("state")
    base = tm // 4 * 4
    member = tm % 4
    p = member // 2
    h = member % 2
    me = member * parts + s
    core = s + 1 - 2 * (s % 2)
    over = (s + 2) % 4
    total = 4 * parts

    def device(p_, h_, s_):
        return (base + 2 * p_ + h_, s_)

    loads = [
        pltpu.make_async_copy(src, dst, load.at[k])
        for k, (src, dst) in enumerate(((pattern_hbm, pattern_ref), (emit_hbm, emit_ref), (w_hbm, w_ref)))
    ]
    for k in range(3):
        loads[k].start()

    barrier = pltpu.get_barrier_semaphore()
    for k in range(1, total):
        peer = (me + k) % total
        pl.semaphore_signal(barrier, inc=1, device_id=(base + peer // parts, peer % parts), device_id_type=MESH)

    for k in range(2):
        loads[k].wait()

    restart = 0.0001 + 0.4999 * jnp.full((1, width), boundary_ref[0]).astype(jnp.float32)
    column = lax.broadcasted_iota(jnp.int32, (blocks, width), 1) // BLOCK + s * (width // BLOCK)
    chosen = (column == lax.broadcasted_iota(jnp.int32, (blocks, width), 0)).astype(jnp.float32)
    mine = jnp.dot(pattern_ref[...].astype(jnp.float32), chosen, preferred_element_type=jnp.float32)
    aux_ref[...] = mine * (4.0 * (1.0 - restart) / restart)
    info[:, 0:width] = emit_ref[...]
    info[:, width:width + BLOCK] = jnp.log(restart / states)[:, 0:BLOCK]

    pl.semaphore_wait(barrier, total - 1)

    def info_copy(k):
        peer = (me + k) % total
        return pltpu.make_async_remote_copy(
            src_ref=info, dst_ref=infos.at[me], send_sem=info_send.at[0], recv_sem=info_recv.at[0],
            device_id=(base + peer // parts, peer % parts), device_id_type=MESH)

    loads[2].wait()
    infos[me] = info[...]

    def remote(src, dst, send, recv, target):
        return pltpu.make_async_remote_copy(
            src_ref=src, dst_ref=dst, send_sem=send, recv_sem=recv, device_id=target, device_id_type=MESH)

    def same(view, send, recv, target):
        return remote(view, view, send, recv, target)

    def fine_row(i):
        return pl.multiple_of(i * FINE, FINE)

    def local_row(g):
        return pl.multiple_of(g * ROWS, ROWS)

    def half_rows(i, side):
        return pl.multiple_of(((2 + side - 2 * (i // per_quarter)) * per_quarter + i % per_quarter) * ROWS, ROWS)

    def columns(n):
        return pl.ds(n * strip, strip)

    def piece_rows(j):
        return pl.ds(j * piece, piece)

    def x_copy(i, row, count):
        recv = p_recv if count == FINE else x_recv
        return same(left.at[s, pl.ds(row, count)], x_send.at[0], recv.at[i], device(p, 1 - h, s))

    def y_over(i, row, count, slot):
        return same(left.at[slot, pl.ds(row, count)], y_send.at[1], y_recv.at[i], device(p, h, over))

    def y_core(kind, i, row, count, slot):
        return same(left.at[slot, pl.ds(row, count)], y_send.at[kind], c_recv.at[i], device(p, h, core))

    def pair_copy(kind, i, target):
        return same(pair.at[pl.ds(fine_row(i), FINE)], p_send.at[kind], p_recv.at[i], target)

    def g_over(g, slot):
        return same(first.at[slot, pl.ds(local_row(g), ROWS)], g_send.at[1], y_recv.at[fine // 2 + g], device(p, h, over))

    def g_core(kind, g, slot):
        return same(first.at[slot, pl.ds(local_row(g), ROWS)], g_send.at[kind], k_recv.at[0], device(p, h, core))

    def strip_over(n, j, slot):
        view = first.at[slot, piece_rows(j), columns(n)]
        return same(view, g_send.at[1], y_recv.at[fine // 2 + n * PIECES + j], device(p, h, over))

    def strip_core(kind, n, j, slot):
        view = first.at[slot, piece_rows(j), columns(n)]
        return same(view, g_send.at[kind], k_recv.at[n // (STRIPS - 1)], device(p, h, core))

    def q_copy(g):
        rows = pl.ds(local_row(g), ROWS)
        return remote(stage.at[rows], first.at[s, rows], q_send.at[0], w_recv.at[g], device(1 - p, 1, s))

    def q_piece(n, j):
        return remote(
            stage.at[piece_rows(j), columns(n)], first.at[s, piece_rows(j), columns(n)],
            q_send.at[0], y_recv.at[fine * 3 // 4 + n * PIECES + j], device(1 - p, 0, s))

    def w_copy(g):
        return remote(
            stage.at[pl.ds(local_row(g), ROWS)], stage.at[pl.ds(local_row(g + per_quarter), ROWS)],
            w_send.at[0], w_recv.at[g], device(p, h, over))

    def v_copy(g):
        return remote(
            stage.at[pl.ds(local_row(g + per_quarter), ROWS)], first.at[over, pl.ds(local_row(g), ROWS)],
            v_send.at[0], v_recv.at[g], device(1 - p, 1, s))

    def b_copy(n):
        begin = DETOUR * DETOURS if n == STRIPS - 1 else 0
        view = right.at[pl.ds(begin, states - begin), columns(n)]
        return same(view, b_send.at[0], b_recv.at[n], device(p, 1 - h, s))

    def d_copy(k, target):
        view = right.at[pl.ds(k * DETOUR, DETOUR), columns(STRIPS - 1)]
        return same(view, d_send.at[0], d_recv.at[k], target)

    def odds(row, count):
        gain = aux_ref[pl.ds(row // BLOCK, 1), :]
        return 1.0 + w_ref[pl.ds(row, count), :].astype(jnp.float32) * gain

    def loop(count, body, start=0):
        def run(i, c):
            body(i)
            return c
        lax.fori_loop(start, count, run, 0)

    def send_fine(i):
        row = fine_row(i)
        left[s, pl.ds(row, FINE), :] = odds(row, FINE)
        x_copy(i, row, FINE).start()

    def send_half(i):
        row = half_rows(i, 1)
        left[s, pl.ds(row, ROWS), :] = odds(row, ROWS)
        x_copy(i, row, ROWS).start()
        near = half_rows(i, 0)
        left[s, pl.ds(near, ROWS), :] = odds(near, ROWS)
        y_over(i, near, ROWS, s).start()
        y_core(0, i, near, ROWS, s).start()

    @pl.when((h == 0) & (p == 1))
    def _():
        send_fine(0)

    for k in range(1, total):
        info_copy(k).start()

    @pl.when((h == 0) & (p == 1))
    def _():
        loop(fine, send_fine, start=1)

    @pl.when((h == 0) & (p == 0))
    def _():
        loop(half, send_half)

    @pl.when((h == 1) & (p == 1))
    def _():
        @functools.partial(loop, chunks)
        def _(i):
            row = local_row(i)
            trail[pl.ds(row, ROWS), :] = odds(row, ROWS).astype(jnp.bfloat16)

    @pl.when((h == 1) & (p == 0))
    def _():
        def fill(n, low, high):
            @functools.partial(loop, high // ROWS, start=low // ROWS)
            def _(i):
                row = local_row(i)
                gain = aux_ref[pl.ds(row // BLOCK, 1), :][:, n * strip:(n + 1) * strip]
                value = 1.0 + w_ref[pl.ds(row, ROWS), columns(n)].astype(jnp.float32) * gain
                right[pl.ds(row, ROWS), columns(n)] = value
                trail[pl.ds(row, ROWS), columns(n)] = value.astype(jnp.bfloat16)

        fill(STRIPS - 1, 0, DETOUR * DETOURS)
        for k in range(DETOURS):
            d_copy(k, device(1, 0, s)).start()
        for n in range(STRIPS):
            fill(n, DETOUR * DETOURS if n == STRIPS - 1 else 0, states)
            b_copy(n).start()

    def take(i, row, count):
        x_copy(i, row, count).wait_recv()
        y_over(i, row, count, s).start()
        y_core(0, i, row, count, s).start()

    def relay(i, row, count):
        y_over(i, row, count, over).wait_recv()
        y_core(2, i, row, count, over).start()

    def have(i, row, count):
        view = left.at[pl.ds(0, 2), pl.ds(row, count)]
        same(view, y_send.at[0], c_recv.at[i], device(p, h, core)).wait_recv()

    def stream(t):
        @pl.when(t < fine)
        def _():
            take(t, fine_row(t), FINE)

        @pl.when((t >= RELAY) & (t < fine + RELAY))
        def _():
            relay(t - RELAY, fine_row(t - RELAY), FINE)

    @pl.when((p == 1) & (h == 1))
    def _():
        loop(HAVE, stream)

    @pl.when((p == 1) & (h == 0))
    def _():
        for k in range(DETOURS):
            d_copy(k, device(0, 0, s)).wait_recv()
            d_copy(k, device(0, 0, s)).start()

    def near_stream(t):
        @pl.when(t < half)
        def _():
            take(t, half_rows(t, 1), ROWS)

        @pl.when((t >= NEAR_RELAY) & (t < half + NEAR_RELAY))
        def _():
            relay(t - NEAR_RELAY, half_rows(t - NEAR_RELAY, 1), ROWS)

    @pl.when((p == 0) & (h == 1))
    def _():
        loop(NEAR_FIRST, near_stream)

    @pl.when((p == 0) & (h == 0))
    def _():
        @functools.partial(loop, half)
        def _(i):
            relay(i, half_rows(i, 0), ROWS)

    same(infos.at[pl.ds(0, total - 1)], info_send.at[0], info_recv.at[0], device(p, h, core)).wait_recv()

    def emission(m, part):
        return infos[m * parts + part, :, 0:width]

    def peak(m):
        top = emission(m, 0)
        for part in range(1, parts):
            top = jnp.maximum(top, emission(m, part))
        return jnp.max(top, axis=1, keepdims=True)

    left_peak = jnp.where(p == 0, peak(0), peak(2))
    weights = [
        jnp.exp(jnp.where(p == 0, emission(0, part), emission(2, part)) - left_peak) for part in range(parts)
    ]
    middle_peak = peak(1)
    middle_emission = infos[parts + s, :, 0:width]
    middle_scale = jnp.exp(middle_emission - middle_peak) * 2.0 ** LEAD_SHIFT

    def product(row, count, n):
        acc = None
        for part in range(parts):
            lead = (left[part, pl.ds(row, count), :] * weights[part]).astype(jnp.bfloat16)
            block = slice(part * width, (part + 1) * width)
            right_block = trail[block, :] if n is None else trail[block, n * strip:(n + 1) * strip]
            term = jnp.dot(lead, right_block, preferred_element_type=jnp.float32)
            acc = term if acc is None else acc + term
        return acc

    @pl.when((p == 1) & (h == 1))
    def _():
        @functools.partial(loop, fine + HAVE, start=HAVE)
        def _(t):
            stream(t)

            i = t - HAVE
            row = fine_row(i)
            have(i, row, FINE)
            value = product(row, FINE, None) * 2.0 ** TRAIL_SHIFT
            pair[pl.ds(row, FINE), :] = value

            @pl.when(i >= fine - DIRECT)
            def _():
                pair_copy(2, i, device(0, 0, s)).start()

            pair_copy(0, i, device(0, 1, s)).start()
            pair_copy(1, i, device(1, 0, s)).start()
            paired[pl.ds(row, FINE), :] = value.astype(jnp.bfloat16)

            @pl.when((t >= fine - per_quarter) & (t < fine))
            def _():
                g = t - (fine - per_quarter)
                q_copy(g).wait_recv()
                g_core(0, g, s).start()
                v_copy(g).wait_recv()
                g_core(2, g, over).start()

    @pl.when((p == 0) & (h == 1))
    def _():
        @functools.partial(loop, half + NEAR_LATER, start=NEAR_FIRST)
        def _(t):
            near_stream(t)

            @pl.when((t >= NEAR_HAVE) & (t < half + NEAR_HAVE))
            def _():
                i = t - NEAR_HAVE
                g = i % per_quarter
                row = half_rows(i, 1)
                have(i, row, ROWS)
                value = product(row, ROWS, None) * middle_scale

                @pl.when(i < per_quarter)
                def _():
                    stage[pl.ds(local_row(g), ROWS), :] = value
                    w_copy(g).start()
                    q_copy(g).start()

                @pl.when(i >= per_quarter)
                def _():
                    first[s, pl.ds(local_row(g), ROWS), :] = value
                    g_over(g, s).start()
                    g_core(0, g, s).start()

            @pl.when(t >= NEAR_LATER)
            def _():
                i = t - NEAR_LATER
                g = i % per_quarter

                @pl.when(i < per_quarter)
                def _():
                    w_copy(g).wait_recv()
                    v_copy(g).start()

                @pl.when(i >= per_quarter)
                def _():
                    g_over(g, over).wait_recv()
                    g_core(2, g, over).start()

    unit = states // 16
    tile = quarter_rows // 4

    def partial_sum(row, ranges):
        acc = None
        for low, high in ranges:
            part, begin = low * unit // width, low * unit % width
            lead = first[part, pl.ds(row, tile), begin:begin + (high - low) * unit].astype(jnp.bfloat16)
            term = jnp.dot(lead, paired[low * unit:high * unit, :], preferred_element_type=jnp.float32)
            acc = term if acc is None else acc + term
        return acc

    def early_sum(i):
        row = pl.multiple_of(i * tile, tile)
        out_ref[pl.ds(row, tile), :] = partial_sum(row, EARLY)

    def middle_sum(i):
        row = pl.multiple_of(i * tile, tile)
        out_ref[pl.ds(row, tile), :] += partial_sum(row, MIDDLE)

    def wait_core(low, high, k):
        view = first.at[pl.ds(0, 2), :, pl.ds(low, high - low)]
        same(view, g_send.at[0], k_recv.at[k], device(p, h, core)).wait_recv()

    def strip_out(n, j):
        strip_over(n, j, s).start()
        strip_core(0, n, j, s).start()

    def strip_relay(n, j):
        strip_over(n, j, over).wait_recv()
        strip_core(2, n, j, over).start()

    def arrive(i):
        pair_copy(0, i, device(0, h, s)).wait_recv()

    def round_pair(i):
        row = fine_row(i)
        paired[pl.ds(row, FINE), :] = pair[pl.ds(row, FINE), :].astype(jnp.bfloat16)

    def relay_pair(i):
        arrive(i)

        @pl.when(i < fine - DIRECT)
        def _():
            pair_copy(0, i, device(0, 0, s)).start()

        round_pair(i)

    def strip_arrive(n, j):
        q_piece(n, j).wait_recv()
        strip_out(n, j)

    @pl.when((p == 1) & (h == 0))
    def _():
        for low, high, arrival, passing, part_row in SCHEDULE:
            loop(fine * high // 64, relay_pair, start=fine * low // 64)
            for j in range(PIECES):
                if arrival is not None:
                    strip_arrive(arrival, j)
                if passing is not None:
                    strip_relay(passing, j)
            if part_row == 0:
                wait_core(0, width - strip, 0)
            if part_row is not None:
                early_sum(part_row)
        done = 56
        for high, arrival, passing in LAST_SCHEDULE:
            loop(fine * high // 64, relay_pair, start=fine * done // 64)
            done = high
            if arrival is not None:
                strip_arrive(STRIPS - 1, arrival)
            if passing is not None:
                strip_relay(STRIPS - 1, passing)
        loop(fine * 63 // 64, relay_pair, start=fine * done // 64)

    @pl.when((p == 0) & (h == 0))
    def _():
        @functools.partial(loop, half)
        def _(i):
            have(i, half_rows(i, 0), ROWS)

        for n in range(STRIPS):
            b_copy(n).wait_recv()
            if n == STRIPS - 1:
                for k in range(DETOURS):
                    d_copy(k, device(1, 0, s)).wait_recv()

            @functools.partial(loop, chunks)
            def _(i):
                row = local_row(i)
                trail[pl.ds(row, ROWS), columns(n)] = right[pl.ds(row, ROWS), columns(n)].astype(jnp.bfloat16)

            scale = middle_scale[:, n * strip:(n + 1) * strip]
            for j in range(PIECES):
                stage[piece_rows(j), columns(n)] = product(2 * quarter_rows + j * piece, piece, n) * scale
                q_piece(n, j).start()
            for j in range(PIECES):
                first[s, piece_rows(j), columns(n)] = product(j * piece, piece, n) * scale
                strip_out(n, j)
            if n > 0:
                for j in range(PIECES):
                    strip_relay(n - 1, j)
        for j in range(PIECES):
            strip_relay(STRIPS - 1, j)

    first_cut = fine * 12 // 16
    second_cut = fine * 15 // 16

    def bring(low, high):
        def run(i, c):
            arrive(i)
            round_pair(i)
            return c
        lax.fori_loop(low, high, run, 0)

    @pl.when(p == 0)
    def _():
        bring(0, first_cut)

    @pl.when(h == 1)
    def _():
        wait_core(0, width, 0)
        loop(4, early_sum)

    @pl.when((h == 0) & (p == 0))
    def _():
        wait_core(0, width - strip, 0)
        loop(4, early_sum)

    @pl.when(h == 0)
    def _():
        wait_core(width - strip, width, 1)

    @pl.when(p == 0)
    def _():
        bring(first_cut, second_cut)

    loop(4, middle_sum)

    log_shares = jnp.zeros((1, 1), jnp.float32)
    for m in range(4):
        log_shares += infos[m * parts, :, width:width + 1]
    shift = math.log(2.0) * (LEAD_SHIFT + TRAIL_SHIFT)
    last_emission = jnp.zeros_like(middle_emission)
    for part in range(parts):
        last_emission = jnp.where(s == part, emission(3, part), last_emission)
    offset = last_emission + log_shares + (peak(0) + middle_peak + peak(2) - shift)

    offset_ref[...] = offset

    @pl.when(p == 0)
    def _():
        bring(second_cut, fine)

    @pl.when((p == 1) & (h == 0))
    def _():
        loop(fine, relay_pair, start=fine * 63 // 64)

    def store(i):
        rows = pl.ds(pl.multiple_of(i * tile, tile), tile)
        return pltpu.make_async_copy(out_ref.at[rows], out_hbm.at[rows], o_send.at[i])

    @functools.partial(loop, 4)
    def _(i):
        row = pl.multiple_of(i * tile, tile)
        out_ref[pl.ds(row, tile), :] += partial_sum(row, FINAL)
        store(i).start()

    same(infos.at[pl.ds(0, total - 1)], info_send.at[0], info_recv.at[0], device(p, h, core)).wait_send()

    def sent(view, sem):
        same(view, sem, load.at[0], device(p, h, core)).wait_send()

    def sent_left(count):
        for kind in range(3):
            sent(left.at[0, pl.ds(0, count)], y_send.at[kind])

    sent(first.at[0], g_send.at[0])
    sent(first.at[0], g_send.at[2])

    @pl.when((p == 0) | (h == 0))
    def _():
        sent(first.at[0], g_send.at[1])

    @pl.when((p == 1) & (h == 1))
    def _():
        sent_left(states)
        sent(pair, p_send.at[0])
        sent(pair, p_send.at[1])
        sent(pair.at[pl.ds(0, DIRECT * FINE)], p_send.at[2])

    @pl.when((p == 1) & (h == 0))
    def _():
        sent(left.at[0], x_send.at[0])
        sent(pair.at[pl.ds(0, states - DIRECT * FINE)], p_send.at[0])
        sent(right.at[pl.ds(0, DETOUR * DETOURS), columns(0)], d_send.at[0])

    @pl.when((p == 0) & (h == 1))
    def _():
        sent(right.at[pl.ds(0, states - DETOUR * DETOURS // STRIPS)], b_send.at[0])
        sent(right.at[pl.ds(0, DETOUR * DETOURS), columns(0)], d_send.at[0])
        sent_left(half_states)
        sent(stage.at[pl.ds(0, quarter_rows)], q_send.at[0])
        sent(stage.at[pl.ds(0, quarter_rows)], w_send.at[0])
        sent(stage.at[pl.ds(0, quarter_rows)], v_send.at[0])

    @pl.when((p == 0) & (h == 0))
    def _():
        sent(left.at[0, pl.ds(0, half_states)], x_send.at[0])
        sent_left(half_states)
        sent(stage.at[pl.ds(0, quarter_rows)], q_send.at[0])

    for i in range(4):
        store(i).wait()


def on_device(parts, trans_weight, pattern, boundary, log_emit):
    weight = trans_weight[0]
    states, width = weight.shape
    blocks = pattern.shape[0]
    fine = states // FINE
    groups = states // ROWS // 4
    dma = pltpu.SemaphoreType.DMA
    hbm = pl.BlockSpec(memory_space=pl.ANY)
    total, offset = pl.pallas_call(
        functools.partial(kernel, parts),
        out_shape=(
            jax.ShapeDtypeStruct((states // 4, width), jnp.float32), jax.ShapeDtypeStruct((1, width), jnp.float32),
        ),
        in_specs=[hbm, hbm, pl.BlockSpec(memory_space=pltpu.SMEM), hbm],
        out_specs=(hbm, pl.BlockSpec(memory_space=pltpu.VMEM)),
        scratch_shapes=[
            pltpu.VMEM((states // 4, width), jnp.float32),
            pltpu.VMEM((states, width), jnp.bfloat16),
            pltpu.VMEM((blocks, blocks), jnp.int32),
            pltpu.VMEM((1, width), jnp.float32),
            pltpu.VMEM((blocks, width), jnp.float32),
            pltpu.VMEM((1, width + BLOCK), jnp.float32),
            pltpu.VMEM((parts, states, width), jnp.float32),
            pltpu.VMEM((states, width), jnp.bfloat16),
            pltpu.VMEM((states, width), jnp.float32),
            pltpu.VMEM((states, width), jnp.bfloat16),
            pltpu.VMEM((parts, states // 4, width), jnp.float32),
            pltpu.VMEM((states // 2, width), jnp.float32),
            pltpu.VMEM((states, width), jnp.float32),
            pltpu.VMEM((4 * parts, 1, width + BLOCK), jnp.float32),
            dma((3,)), dma((1,)), dma((1,)),
            dma((1,)), dma((states // ROWS // 2,)),
            dma((3,)), dma((fine,)), dma((fine,)),
            dma((3,)), dma((fine,)),
            dma((1,)), dma((3,)), dma((2,)),
            dma((1,)), dma((STRIPS,)),
            dma((1,)), dma((groups,)), dma((1,)), dma((groups,)), dma((1,)), dma((DETOURS,)), dma((4,)),
        ],
        compiler_params=pltpu.CompilerParams(
            collective_id=0, has_side_effects=True, vmem_limit_bytes=52 * 1024 * 1024
        ),
    )(weight, pattern, boundary, log_emit)
    return jnp.log(total) + offset


def solution(mesh):
    return jax.shard_map(
        functools.partial(on_device, mesh.shape["state"]),
        mesh=mesh,
        in_specs=(P("tm", None, "state"), P(), P("tm"), P("tm", "state")),
        out_specs=P("tm", "state"),
        check_vma=False,
    )
```

```python
import functools
import math

import jax
import jax.numpy as jnp
from jax import lax
from jax.experimental import pallas as pl
from jax.experimental.pallas import tpu as pltpu
from jax.sharding import PartitionSpec as P

BLOCK = 128
ROWS = 64
FINE = 32
RING = 16
RELAY = 2
HAVE = 3
NEAR_FIRST = 2
NEAR_RELAY = 3
NEAR_HAVE = 4
NEAR_LATER = 8
STRIPS = 4
PIECES = 4
DIRECT = 1
DETOUR = 256
DETOURS = 2
SCHEDULE = (
    (0, 33, 0, None, None), (33, 37, 1, None, None), (37, 39, None, 0, None), (39, 42, None, 1, None),
    (42, 48, 2, None, None), (48, 52, None, 2, None), (52, 53, None, None, 0), (53, 54, None, None, 1),
    (54, 55, None, None, 2), (55, 56, None, None, 3),
)
LAST_SCHEDULE = ((56, 0, None), (57, 1, None), (58, 2, None), (59, 3, 0), (60, None, 1), (61, None, 2), (62, None, 3))
EARLY = ((0, 3), (4, 7), (8, 11))
MIDDLE = ((3, 4), (7, 8), (11, 12), (12, 15))
FINAL = ((15, 16),)
LEAD_SHIFT = 12
TRAIL_SHIFT = -49
MESH = pl.DeviceIdType.MESH


def kernel(
    parts, w_hbm, packed_ref, boundary_ref, out_hbm, offset_ref,
    out_ref,    w_ref, aux_ref, info, left, trail, pair, paired, first, stage, right, infos,
    load, info_send, info_recv, x_send, x_recv, y_send, y_recv, c_recv, p_send, p_recv,
    q_send, g_send, k_recv, b_send, b_recv, w_send, w_recv, v_send, v_recv, d_send, d_recv, o_send,
):
    states, width = w_ref.shape
    blocks = states // BLOCK
    chunks = states // ROWS
    fine = states // FINE
    per_quarter = chunks // 4
    half = chunks // 2
    half_states = states // 2
    quarter_rows = states // 4
    strip = width // STRIPS
    piece = quarter_rows // PIECES
    tm = lax.axis_index("tm")
    s = lax.axis_index("state")
    base = tm // 4 * 4
    member = tm % 4
    p = member // 2
    h = member % 2
    me = member * parts + s
    core = s + 1 - 2 * (s % 2)
    over = (s + 2) % 4
    total = 4 * parts

    def device(p_, h_, s_):
        return (base + 2 * p_ + h_, s_)

    loads = [
        pltpu.make_async_copy(w_hbm.at[pl.ds(low, count)], w_ref.at[pl.ds(low, count)], load.at[k])
        for k, (low, count) in enumerate(((0, BLOCK), (BLOCK, states - BLOCK)))
    ]
    for k in range(2):
        loads[k].start()

    barrier = pltpu.get_barrier_semaphore()
    for k in range(1, total):
        peer = (me + k) % total
        pl.semaphore_signal(barrier, inc=1, device_id=(base + peer // parts, peer % parts), device_id_type=MESH)


    restart = 0.0001 + 0.4999 * jnp.full((1, width), boundary_ref[0]).astype(jnp.float32)
    column = lax.broadcasted_iota(jnp.int32, (blocks, width), 1) // BLOCK + s * (width // BLOCK)
    chosen = (column == lax.broadcasted_iota(jnp.int32, (blocks, width), 0)).astype(jnp.float32)
    mine = jnp.dot(packed_ref[0:blocks, 0:blocks], chosen, preferred_element_type=jnp.float32)
    aux_ref[...] = mine * (4.0 * (1.0 - restart) / restart)
    info[:, 0:width] = packed_ref[blocks:blocks + 1, :]
    info[:, width:width + BLOCK] = jnp.log(restart / states)[:, 0:BLOCK]

    pl.semaphore_wait(barrier, total - 1)

    def info_copy(k):
        peer = (me + k) % total
        return pltpu.make_async_remote_copy(
            src_ref=info, dst_ref=infos.at[me], send_sem=info_send.at[0], recv_sem=info_recv.at[0],
            device_id=(base + peer // parts, peer % parts), device_id_type=MESH)

    loads[0].wait()
    infos[me] = info[...]

    def remote(src, dst, send, recv, target):
        return pltpu.make_async_remote_copy(
            src_ref=src, dst_ref=dst, send_sem=send, recv_sem=recv, device_id=target, device_id_type=MESH)

    def same(view, send, recv, target):
        return remote(view, view, send, recv, target)

    def fine_row(i):
        return pl.multiple_of(i * FINE, FINE)

    def local_row(g):
        return pl.multiple_of(g * ROWS, ROWS)

    def half_rows(i, side):
        return pl.multiple_of(((2 + side - 2 * (i // per_quarter)) * per_quarter + i % per_quarter) * ROWS, ROWS)

    def columns(n):
        return pl.ds(n * strip, strip)

    def piece_rows(j):
        return pl.ds(j * piece, piece)

    def x_copy(i, row, count):
        recv = p_recv if count == FINE else x_recv
        return same(left.at[s, pl.ds(row, count)], x_send.at[0], recv.at[i], device(p, 1 - h, s))

    def y_over(i, row, count, slot):
        return same(left.at[slot, pl.ds(row, count)], y_send.at[1], y_recv.at[i % RING], device(p, h, over))

    def y_core(kind, i, row, count, slot):
        return same(left.at[slot, pl.ds(row, count)], y_send.at[kind], c_recv.at[i % RING], device(p, h, core))

    def pair_copy(kind, i, target):
        return same(pair.at[pl.ds(fine_row(i), FINE)], p_send.at[kind], p_recv.at[i], target)

    def g_over(g, slot):
        return same(first.at[slot, pl.ds(local_row(g), ROWS)], g_send.at[1], y_recv.at[RING + g], device(p, h, over))

    def g_core(kind, g, slot):
        return same(first.at[slot, pl.ds(local_row(g), ROWS)], g_send.at[kind], k_recv.at[0], device(p, h, core))

    def strip_over(n, j, slot):
        view = first.at[slot, piece_rows(j), columns(n)]
        return same(view, g_send.at[1], y_recv.at[RING + n * PIECES + j], device(p, h, over))

    def strip_core(kind, n, j, slot):
        view = first.at[slot, piece_rows(j), columns(n)]
        return same(view, g_send.at[kind], k_recv.at[n // (STRIPS - 1)], device(p, h, core))

    def q_copy(g):
        rows = pl.ds(local_row(g), ROWS)
        return remote(stage.at[rows], first.at[s, rows], q_send.at[0], w_recv.at[g], device(1 - p, 1, s))

    def q_piece(n, j):
        return remote(
            stage.at[piece_rows(j), columns(n)], first.at[s, piece_rows(j), columns(n)],
            q_send.at[0], y_recv.at[n * PIECES + j], device(1 - p, 0, s))

    def w_copy(g):
        return remote(
            stage.at[pl.ds(local_row(g), ROWS)], stage.at[pl.ds(local_row(g + per_quarter), ROWS)],
            w_send.at[0], w_recv.at[g], device(p, h, over))

    def v_copy(g):
        return remote(
            stage.at[pl.ds(local_row(g + per_quarter), ROWS)], first.at[over, pl.ds(local_row(g), ROWS)],
            v_send.at[0], v_recv.at[g], device(1 - p, 1, s))

    def b_copy(n):
        begin = DETOUR * DETOURS if n == STRIPS - 1 else 0
        view = right.at[pl.ds(begin, states - begin), columns(n)]
        return same(view, b_send.at[0], b_recv.at[n], device(p, 1 - h, s))

    def d_copy(k, target):
        view = right.at[pl.ds(k * DETOUR, DETOUR), columns(STRIPS - 1)]
        return same(view, d_send.at[0], d_recv.at[k], target)

    def odds(row, count):
        gain = aux_ref[pl.ds(row // BLOCK, 1), :]
        return 1.0 + w_ref[pl.ds(row, count), :].astype(jnp.float32) * gain

    def loop(count, body, start=0):
        def run(i, c):
            body(i)
            return c
        lax.fori_loop(start, count, run, 0)

    def send_fine(i):
        row = fine_row(i)
        left[s, pl.ds(row, FINE), :] = odds(row, FINE)
        x_copy(i, row, FINE).start()

    def send_half(i):
        row = half_rows(i, 1)
        left[s, pl.ds(row, ROWS), :] = odds(row, ROWS)
        x_copy(i, row, ROWS).start()
        near = half_rows(i, 0)
        left[s, pl.ds(near, ROWS), :] = odds(near, ROWS)
        y_over(i, near, ROWS, s).start()
        y_core(0, i, near, ROWS, s).start()

    @pl.when((h == 0) & (p == 1))
    def _():
        send_fine(0)

    for k in range(1, total):
        info_copy(k).start()
    loads[1].wait()

    @pl.when((h == 0) & (p == 1))
    def _():
        loop(fine, send_fine, start=1)

    @pl.when((h == 0) & (p == 0))
    def _():
        loop(half, send_half)

    @pl.when((h == 1) & (p == 1))
    def _():
        @functools.partial(loop, chunks)
        def _(i):
            row = local_row(i)
            trail[pl.ds(row, ROWS), :] = odds(row, ROWS).astype(jnp.bfloat16)

    @pl.when((h == 1) & (p == 0))
    def _():
        def fill(n, low, high):
            @functools.partial(loop, high // ROWS, start=low // ROWS)
            def _(i):
                row = local_row(i)
                gain = aux_ref[pl.ds(row // BLOCK, 1), :][:, n * strip:(n + 1) * strip]
                value = 1.0 + w_ref[pl.ds(row, ROWS), columns(n)].astype(jnp.float32) * gain
                right[pl.ds(row, ROWS), columns(n)] = value
                trail[pl.ds(row, ROWS), columns(n)] = value.astype(jnp.bfloat16)

        fill(STRIPS - 1, 0, DETOUR * DETOURS)
        for k in range(DETOURS):
            d_copy(k, device(1, 0, s)).start()
        for n in range(STRIPS):
            fill(n, DETOUR * DETOURS if n == STRIPS - 1 else 0, states)
            b_copy(n).start()

    def take(i, row, count):
        x_copy(i, row, count).wait_recv()
        y_over(i, row, count, s).start()
        y_core(0, i, row, count, s).start()

    def relay(i, row, count):
        y_over(i, row, count, over).wait_recv()
        y_core(2, i, row, count, over).start()

    def have(i, row, count):
        view = left.at[pl.ds(0, 2), pl.ds(row, count)]
        same(view, y_send.at[0], c_recv.at[i % RING], device(p, h, core)).wait_recv()

    def stream(t):
        @pl.when(t < fine)
        def _():
            take(t, fine_row(t), FINE)

        @pl.when((t >= RELAY) & (t < fine + RELAY))
        def _():
            relay(t - RELAY, fine_row(t - RELAY), FINE)

    @pl.when((p == 1) & (h == 1))
    def _():
        loop(HAVE, stream)

    @pl.when((p == 1) & (h == 0))
    def _():
        for k in range(DETOURS):
            d_copy(k, device(0, 0, s)).wait_recv()
            d_copy(k, device(0, 0, s)).start()

    def near_stream(t):
        @pl.when(t < half)
        def _():
            take(t, half_rows(t, 1), ROWS)

        @pl.when((t >= NEAR_RELAY) & (t < half + NEAR_RELAY))
        def _():
            relay(t - NEAR_RELAY, half_rows(t - NEAR_RELAY, 1), ROWS)

    @pl.when((p == 0) & (h == 1))
    def _():
        loop(NEAR_FIRST, near_stream)

    @pl.when((p == 0) & (h == 0))
    def _():
        @functools.partial(loop, half)
        def _(i):
            relay(i, half_rows(i, 0), ROWS)

    same(infos.at[pl.ds(0, total - 1)], info_send.at[0], info_recv.at[0], device(p, h, core)).wait_recv()

    def emission(m, part):
        return infos[m * parts + part, :, 0:width]

    def peak(m):
        top = emission(m, 0)
        for part in range(1, parts):
            top = jnp.maximum(top, emission(m, part))
        return jnp.max(top, axis=1, keepdims=True)

    left_peak = jnp.where(p == 0, peak(0), peak(2))
    weights = [
        jnp.exp(jnp.where(p == 0, emission(0, part), emission(2, part)) - left_peak) for part in range(parts)
    ]
    middle_peak = peak(1)
    middle_emission = infos[parts + s, :, 0:width]
    middle_scale = jnp.exp(middle_emission - middle_peak) * 2.0 ** LEAD_SHIFT

    def product(row, count, n):
        acc = None
        for part in range(parts):
            lead = (left[part, pl.ds(row, count), :] * weights[part]).astype(jnp.bfloat16)
            block = slice(part * width, (part + 1) * width)
            right_block = trail[block, :] if n is None else trail[block, n * strip:(n + 1) * strip]
            term = jnp.dot(lead, right_block, preferred_element_type=jnp.float32)
            acc = term if acc is None else acc + term
        return acc

    @pl.when((p == 1) & (h == 1))
    def _():
        @functools.partial(loop, fine + HAVE, start=HAVE)
        def _(t):
            stream(t)

            i = t - HAVE
            row = fine_row(i)
            have(i, row, FINE)
            value = product(row, FINE, None) * 2.0 ** TRAIL_SHIFT
            pair[pl.ds(row, FINE), :] = value

            @pl.when(i >= fine - DIRECT)
            def _():
                pair_copy(2, i, device(0, 0, s)).start()

            pair_copy(0, i, device(0, 1, s)).start()
            pair_copy(1, i, device(1, 0, s)).start()
            paired[pl.ds(row, FINE), :] = value.astype(jnp.bfloat16)

            @pl.when((t >= fine - per_quarter) & (t < fine))
            def _():
                g = t - (fine - per_quarter)
                q_copy(g).wait_recv()
                g_core(0, g, s).start()
                v_copy(g).wait_recv()
                g_core(2, g, over).start()

    @pl.when((p == 0) & (h == 1))
    def _():
        @functools.partial(loop, half + NEAR_LATER, start=NEAR_FIRST)
        def _(t):
            near_stream(t)

            @pl.when((t >= NEAR_HAVE) & (t < half + NEAR_HAVE))
            def _():
                i = t - NEAR_HAVE
                g = i % per_quarter
                row = half_rows(i, 1)
                have(i, row, ROWS)
                value = product(row, ROWS, None) * middle_scale

                @pl.when(i < per_quarter)
                def _():
                    stage[pl.ds(local_row(g), ROWS), :] = value
                    w_copy(g).start()
                    q_copy(g).start()

                @pl.when(i >= per_quarter)
                def _():
                    first[s, pl.ds(local_row(g), ROWS), :] = value
                    g_over(g, s).start()
                    g_core(0, g, s).start()

            @pl.when(t >= NEAR_LATER)
            def _():
                i = t - NEAR_LATER
                g = i % per_quarter

                @pl.when(i < per_quarter)
                def _():
                    w_copy(g).wait_recv()
                    v_copy(g).start()

                @pl.when(i >= per_quarter)
                def _():
                    g_over(g, over).wait_recv()
                    g_core(2, g, over).start()

    unit = states // 16
    tile = quarter_rows // 4

    def partial_sum(row, ranges):
        acc = None
        for low, high in ranges:
            part, begin = low * unit // width, low * unit % width
            lead = first[part, pl.ds(row, tile), begin:begin + (high - low) * unit].astype(jnp.bfloat16)
            term = jnp.dot(lead, paired[low * unit:high * unit, :], preferred_element_type=jnp.float32)
            acc = term if acc is None else acc + term
        return acc

    def early_sum(i):
        row = pl.multiple_of(i * tile, tile)
        out_ref[pl.ds(row, tile), :] = partial_sum(row, EARLY)

    def middle_sum(i):
        row = pl.multiple_of(i * tile, tile)
        out_ref[pl.ds(row, tile), :] += partial_sum(row, MIDDLE)

    def wait_core(low, high, k):
        view = first.at[pl.ds(0, 2), :, pl.ds(low, high - low)]
        same(view, g_send.at[0], k_recv.at[k], device(p, h, core)).wait_recv()

    def strip_out(n, j):
        strip_over(n, j, s).start()
        strip_core(0, n, j, s).start()

    def strip_relay(n, j):
        strip_over(n, j, over).wait_recv()
        strip_core(2, n, j, over).start()

    def arrive(i):
        pair_copy(0, i, device(0, h, s)).wait_recv()

    def round_pair(i):
        row = fine_row(i)
        paired[pl.ds(row, FINE), :] = pair[pl.ds(row, FINE), :].astype(jnp.bfloat16)

    def relay_pair(i):
        arrive(i)

        @pl.when(i < fine - DIRECT)
        def _():
            pair_copy(0, i, device(0, 0, s)).start()

        round_pair(i)

    def strip_arrive(n, j):
        q_piece(n, j).wait_recv()
        strip_out(n, j)

    @pl.when((p == 1) & (h == 0))
    def _():
        for low, high, arrival, passing, part_row in SCHEDULE:
            loop(fine * high // 64, relay_pair, start=fine * low // 64)
            for j in range(PIECES):
                if arrival is not None:
                    strip_arrive(arrival, j)
                if passing is not None:
                    strip_relay(passing, j)
            if part_row == 0:
                wait_core(0, width - strip, 0)
            if part_row is not None:
                early_sum(part_row)
        done = 56
        for high, arrival, passing in LAST_SCHEDULE:
            loop(fine * high // 64, relay_pair, start=fine * done // 64)
            done = high
            if arrival is not None:
                strip_arrive(STRIPS - 1, arrival)
            if passing is not None:
                strip_relay(STRIPS - 1, passing)
        loop(fine * 63 // 64, relay_pair, start=fine * done // 64)

    @pl.when((p == 0) & (h == 0))
    def _():
        @functools.partial(loop, half)
        def _(i):
            have(i, half_rows(i, 0), ROWS)

        for n in range(STRIPS):
            b_copy(n).wait_recv()
            if n == STRIPS - 1:
                for k in range(DETOURS):
                    d_copy(k, device(1, 0, s)).wait_recv()

            @functools.partial(loop, chunks)
            def _(i):
                row = local_row(i)
                trail[pl.ds(row, ROWS), columns(n)] = right[pl.ds(row, ROWS), columns(n)].astype(jnp.bfloat16)

            scale = middle_scale[:, n * strip:(n + 1) * strip]
            for j in range(PIECES):
                stage[piece_rows(j), columns(n)] = product(2 * quarter_rows + j * piece, piece, n) * scale
                q_piece(n, j).start()
            for j in range(PIECES):
                first[s, piece_rows(j), columns(n)] = product(j * piece, piece, n) * scale
                strip_out(n, j)
            if n > 0:
                for j in range(PIECES):
                    strip_relay(n - 1, j)
        for j in range(PIECES):
            strip_relay(STRIPS - 1, j)

    first_cut = fine * 12 // 16
    second_cut = fine * 15 // 16

    def bring(low, high):
        def run(i, c):
            arrive(i)
            round_pair(i)
            return c
        lax.fori_loop(low, high, run, 0)

    @pl.when(p == 0)
    def _():
        bring(0, first_cut)

    @pl.when(h == 1)
    def _():
        wait_core(0, width, 0)
        loop(4, early_sum)

    @pl.when((h == 0) & (p == 0))
    def _():
        wait_core(0, width - strip, 0)
        loop(4, early_sum)

    @pl.when(h == 0)
    def _():
        wait_core(width - strip, width, 1)

    @pl.when(p == 0)
    def _():
        bring(first_cut, second_cut)

    loop(4, middle_sum)

    log_shares = jnp.zeros((1, 1), jnp.float32)
    for m in range(4):
        log_shares += infos[m * parts, :, width:width + 1]
    shift = math.log(2.0) * (LEAD_SHIFT + TRAIL_SHIFT)
    last_emission = jnp.zeros_like(middle_emission)
    for part in range(parts):
        last_emission = jnp.where(s == part, emission(3, part), last_emission)
    offset = last_emission + log_shares + (peak(0) + middle_peak + peak(2) - shift)

    offset_ref[...] = offset

    @pl.when(p == 0)
    def _():
        bring(second_cut, fine)

    @pl.when((p == 1) & (h == 0))
    def _():
        loop(fine, relay_pair, start=fine * 63 // 64)

    def store(i):
        rows = pl.ds(pl.multiple_of(i * tile, tile), tile)
        return pltpu.make_async_copy(out_ref.at[rows], out_hbm.at[rows], o_send.at[i])

    @functools.partial(loop, 4)
    def _(i):
        row = pl.multiple_of(i * tile, tile)
        out_ref[pl.ds(row, tile), :] += partial_sum(row, FINAL)
        store(i).start()

    same(infos.at[pl.ds(0, total - 1)], info_send.at[0], info_recv.at[0], device(p, h, core)).wait_send()

    def sent(view, sem):
        same(view, sem, load.at[0], device(p, h, core)).wait_send()

    def sent_left(count):
        for kind in range(3):
            sent(left.at[0, pl.ds(0, count)], y_send.at[kind])

    sent(first.at[0], g_send.at[0])
    sent(first.at[0], g_send.at[2])

    @pl.when((p == 0) | (h == 0))
    def _():
        sent(first.at[0], g_send.at[1])

    @pl.when((p == 1) & (h == 1))
    def _():
        sent_left(states)
        sent(pair, p_send.at[0])
        sent(pair, p_send.at[1])
        sent(pair.at[pl.ds(0, DIRECT * FINE)], p_send.at[2])

    @pl.when((p == 1) & (h == 0))
    def _():
        sent(left.at[0], x_send.at[0])
        sent(pair.at[pl.ds(0, states - DIRECT * FINE)], p_send.at[0])
        sent(right.at[pl.ds(0, DETOUR * DETOURS), columns(0)], d_send.at[0])

    @pl.when((p == 0) & (h == 1))
    def _():
        sent(right.at[pl.ds(0, states - DETOUR * DETOURS // STRIPS)], b_send.at[0])
        sent(right.at[pl.ds(0, DETOUR * DETOURS), columns(0)], d_send.at[0])
        sent_left(half_states)
        sent(stage.at[pl.ds(0, quarter_rows)], q_send.at[0])
        sent(stage.at[pl.ds(0, quarter_rows)], w_send.at[0])
        sent(stage.at[pl.ds(0, quarter_rows)], v_send.at[0])

    @pl.when((p == 0) & (h == 0))
    def _():
        sent(left.at[0, pl.ds(0, half_states)], x_send.at[0])
        sent_left(half_states)
        sent(stage.at[pl.ds(0, quarter_rows)], q_send.at[0])

    for i in range(4):
        store(i).wait()


def on_device(parts, trans_weight, pattern, boundary, log_emit):
    weight = trans_weight[0]
    states, width = weight.shape
    blocks = pattern.shape[0]
    packed = jnp.pad(pattern, ((0, 1), (0, width - blocks))).astype(jnp.float32) + jnp.pad(log_emit, ((blocks, 0), (0, 0)))
    fine = states // FINE
    groups = states // ROWS // 4
    dma = pltpu.SemaphoreType.DMA
    hbm = pl.BlockSpec(memory_space=pl.ANY)
    vmem = pl.BlockSpec(memory_space=pltpu.VMEM)
    total, offset = pl.pallas_call(
        functools.partial(kernel, parts),
        out_shape=(
            jax.ShapeDtypeStruct((states // 4, width), jnp.float32), jax.ShapeDtypeStruct((1, width), jnp.float32),
        ),
        in_specs=[hbm, vmem, pl.BlockSpec(memory_space=pltpu.SMEM)],
        out_specs=(hbm, vmem),
        scratch_shapes=[
            pltpu.VMEM((states // 4, width), jnp.float32),
            pltpu.VMEM((states, width), jnp.bfloat16),
            pltpu.VMEM((blocks, width), jnp.float32),
            pltpu.VMEM((1, width + BLOCK), jnp.float32),
            pltpu.VMEM((parts, states, width), jnp.float32),
            pltpu.VMEM((states, width), jnp.bfloat16),
            pltpu.VMEM((states, width), jnp.float32),
            pltpu.VMEM((states, width), jnp.bfloat16),
            pltpu.VMEM((parts, states // 4, width), jnp.float32),
            pltpu.VMEM((states // 2, width), jnp.float32),
            pltpu.VMEM((states, width), jnp.float32),
            pltpu.VMEM((4 * parts, 1, width + BLOCK), jnp.float32),
            dma((2,)), dma((1,)), dma((1,)),
            dma((1,)), dma((states // ROWS // 2,)),
            dma((3,)), dma((RING + max(groups, STRIPS * PIECES),)), dma((RING,)),
            dma((3,)), dma((fine,)),
            dma((1,)), dma((3,)), dma((2,)),
            dma((1,)), dma((STRIPS,)),
            dma((1,)), dma((groups,)), dma((1,)), dma((groups,)), dma((1,)), dma((DETOURS,)), dma((4,)),
        ],
        compiler_params=pltpu.CompilerParams(
            collective_id=0, has_side_effects=True, vmem_limit_bytes=52 * 1024 * 1024
        ),
    )(weight, packed, boundary)
    return jnp.log(total) + offset


def solution(mesh):
    return jax.shard_map(
        functools.partial(on_device, mesh.shape["state"]),
        mesh=mesh,
        in_specs=(P("tm", None, "state"), P(), P("tm"), P("tm", "state")),
        out_specs=P("tm", "state"),
        check_vma=False,
    )
```

```python
import functools
import math

import jax
import jax.numpy as jnp
from jax import lax
from jax.experimental import pallas as pl
from jax.experimental.pallas import tpu as pltpu
from jax.sharding import PartitionSpec as P

BLOCK = 128
ROWS = 64
FINE = 32
RING = 16
RELAY = 2
HAVE = 3
NEAR_FIRST = 2
NEAR_RELAY = 3
NEAR_HAVE = 4
NEAR_LATER = 8
STRIPS = 4
PIECES = 4
DIRECT = 1
DETOUR = 256
DETOURS = 2
SCHEDULE = (
    (0, 33, 0, None, None), (33, 37, 1, None, None), (37, 39, None, 0, None), (39, 42, None, 1, None),
    (42, 48, 2, None, None), (48, 52, None, 2, None), (52, 53, None, None, 0), (53, 54, None, None, 1),
    (54, 55, None, None, 2), (55, 56, None, None, 3),
)
LAST_SCHEDULE = ((56, 0, None), (57, 1, None), (58, 2, None), (59, 3, 0), (60, None, 1), (61, None, 2), (62, None, 3))
EARLY = ((0, 3), (4, 7), (8, 11))
MIDDLE = ((3, 4), (7, 8), (11, 12), (12, 15))
FINAL = ((15, 16),)
LEAD_SHIFT = 12
TRAIL_SHIFT = -49
MESH = pl.DeviceIdType.MESH


def kernel(
    parts, w_hbm, packed_ref, boundary_ref, out_hbm, offset_ref,
    out_ref,    w_ref, aux_ref, info, left, trail, pair, paired, first, stage, right, infos,
    load, info_send, info_recv, x_send, x_recv, y_send, y_recv, c_recv, p_send, p_recv,
    q_send, g_send, k_recv, b_send, w_send, v_send, d_send, o_send,
):
    states, width = w_ref.shape
    blocks = states // BLOCK
    chunks = states // ROWS
    fine = states // FINE
    per_quarter = chunks // 4
    half = chunks // 2
    half_states = states // 2
    quarter_rows = states // 4
    strip = width // STRIPS
    piece = quarter_rows // PIECES
    tm = lax.axis_index("tm")
    s = lax.axis_index("state")
    base = tm // 4 * 4
    member = tm % 4
    p = member // 2
    h = member % 2
    me = member * parts + s
    core = s + 1 - 2 * (s % 2)
    over = (s + 2) % 4
    total = 4 * parts

    def device(p_, h_, s_):
        return (base + 2 * p_ + h_, s_)

    loads = [
        pltpu.make_async_copy(w_hbm.at[pl.ds(low, count)], w_ref.at[pl.ds(low, count)], load.at[k])
        for k, (low, count) in enumerate(((0, BLOCK), (BLOCK, states - BLOCK)))
    ]
    for k in range(2):
        loads[k].start()

    barrier = pltpu.get_barrier_semaphore()
    for k in range(1, total):
        peer = (me + k) % total
        pl.semaphore_signal(barrier, inc=1, device_id=(base + peer // parts, peer % parts), device_id_type=MESH)


    restart = 0.0001 + 0.4999 * jnp.full((1, width), boundary_ref[0]).astype(jnp.float32)
    column = lax.broadcasted_iota(jnp.int32, (blocks, width), 1) // BLOCK + s * (width // BLOCK)
    chosen = (column == lax.broadcasted_iota(jnp.int32, (blocks, width), 0)).astype(jnp.float32)
    mine = jnp.dot(packed_ref[0:blocks, 0:blocks], chosen, preferred_element_type=jnp.float32)
    aux_ref[...] = mine * (4.0 * (1.0 - restart) / restart)
    info[:, 0:width] = packed_ref[blocks:blocks + 1, :]
    info[:, width:width + BLOCK] = jnp.log(restart / states)[:, 0:BLOCK]

    pl.semaphore_wait(barrier, total - 1)

    def info_copy(k):
        peer = (me + k) % total
        return pltpu.make_async_remote_copy(
            src_ref=info, dst_ref=infos.at[me], send_sem=info_send.at[0], recv_sem=info_recv.at[0],
            device_id=(base + peer // parts, peer % parts), device_id_type=MESH)

    loads[0].wait()
    infos[me] = info[...]

    def remote(src, dst, send, recv, target):
        return pltpu.make_async_remote_copy(
            src_ref=src, dst_ref=dst, send_sem=send, recv_sem=recv, device_id=target, device_id_type=MESH)

    def same(view, send, recv, target):
        return remote(view, view, send, recv, target)

    def fine_row(i):
        return pl.multiple_of(i * FINE, FINE)

    def local_row(g):
        return pl.multiple_of(g * ROWS, ROWS)

    def half_rows(i, side):
        return pl.multiple_of(((2 + side - 2 * (i // per_quarter)) * per_quarter + i % per_quarter) * ROWS, ROWS)

    def columns(n):
        return pl.ds(n * strip, strip)

    def piece_rows(j):
        return pl.ds(j * piece, piece)

    def x_copy(i, row, count):
        recv = p_recv if count == FINE else x_recv
        return same(left.at[s, pl.ds(row, count)], x_send.at[0], recv.at[i], device(p, 1 - h, s))

    def y_over(i, row, count, slot):
        return same(left.at[slot, pl.ds(row, count)], y_send.at[1], y_recv.at[i % RING], device(p, h, over))

    def y_core(kind, i, row, count, slot):
        return same(left.at[slot, pl.ds(row, count)], y_send.at[kind], c_recv.at[i % RING], device(p, h, core))

    def pair_copy(kind, i, target):
        return same(pair.at[pl.ds(fine_row(i), FINE)], p_send.at[kind], p_recv.at[i], target)

    def g_over(g, slot):
        return same(first.at[slot, pl.ds(local_row(g), ROWS)], g_send.at[1], y_recv.at[RING + g], device(p, h, over))

    def g_core(kind, g, slot):
        return same(first.at[slot, pl.ds(local_row(g), ROWS)], g_send.at[kind], k_recv.at[0], device(p, h, core))

    def strip_over(n, j, slot):
        view = first.at[slot, piece_rows(j), columns(n)]
        return same(view, g_send.at[1], y_recv.at[RING + n * PIECES + j], device(p, h, over))

    def strip_core(kind, n, j, slot):
        view = first.at[slot, piece_rows(j), columns(n)]
        return same(view, g_send.at[kind], k_recv.at[n // (STRIPS - 1)], device(p, h, core))

    def q_copy(g):
        rows = pl.ds(local_row(g), ROWS)
        return remote(stage.at[rows], first.at[s, rows], q_send.at[0], x_recv.at[per_quarter + g], device(1 - p, 1, s))

    def q_piece(n, j):
        return remote(
            stage.at[piece_rows(j), columns(n)], first.at[s, piece_rows(j), columns(n)],
            q_send.at[0], y_recv.at[n * PIECES + j], device(1 - p, 0, s))

    def w_copy(g):
        return remote(
            stage.at[pl.ds(local_row(g), ROWS)], stage.at[pl.ds(local_row(g + per_quarter), ROWS)],
            w_send.at[0], y_recv.at[RING + per_quarter + g], device(p, h, over))

    def v_copy(g):
        return remote(
            stage.at[pl.ds(local_row(g + per_quarter), ROWS)], first.at[over, pl.ds(local_row(g), ROWS)],
            v_send.at[0], x_recv.at[g], device(1 - p, 1, s))

    def b_copy(n):
        begin = DETOUR * DETOURS if n == STRIPS - 1 else 0
        view = right.at[pl.ds(begin, states - begin), columns(n)]
        return same(view, b_send.at[0], x_recv.at[n], device(p, 1 - h, s))

    def d_copy(k, target):
        view = right.at[pl.ds(k * DETOUR, DETOUR), columns(STRIPS - 1)]
        return same(view, d_send.at[0], x_recv.at[STRIPS + k], target)

    def odds(row, count):
        gain = aux_ref[pl.ds(row // BLOCK, 1), :]
        return 1.0 + w_ref[pl.ds(row, count), :].astype(jnp.float32) * gain

    def loop(count, body, start=0):
        def run(i, c):
            body(i)
            return c
        lax.fori_loop(start, count, run, 0)

    def send_fine(i):
        row = fine_row(i)
        left[s, pl.ds(row, FINE), :] = odds(row, FINE)
        x_copy(i, row, FINE).start()

    def send_half(i):
        row = half_rows(i, 1)
        left[s, pl.ds(row, ROWS), :] = odds(row, ROWS)
        x_copy(i, row, ROWS).start()
        near = half_rows(i, 0)
        left[s, pl.ds(near, ROWS), :] = odds(near, ROWS)
        y_over(i, near, ROWS, s).start()
        y_core(0, i, near, ROWS, s).start()

    @pl.when((h == 0) & (p == 1))
    def _():
        send_fine(0)

    for k in range(1, total):
        info_copy(k).start()
    loads[1].wait()

    @pl.when((h == 0) & (p == 1))
    def _():
        loop(fine, send_fine, start=1)

    @pl.when((h == 0) & (p == 0))
    def _():
        loop(half, send_half)

    @pl.when((h == 1) & (p == 1))
    def _():
        @functools.partial(loop, chunks)
        def _(i):
            row = local_row(i)
            trail[pl.ds(row, ROWS), :] = odds(row, ROWS).astype(jnp.bfloat16)

    @pl.when((h == 1) & (p == 0))
    def _():
        def fill(n, low, high):
            @functools.partial(loop, high // ROWS, start=low // ROWS)
            def _(i):
                row = local_row(i)
                gain = aux_ref[pl.ds(row // BLOCK, 1), :][:, n * strip:(n + 1) * strip]
                value = 1.0 + w_ref[pl.ds(row, ROWS), columns(n)].astype(jnp.float32) * gain
                right[pl.ds(row, ROWS), columns(n)] = value
                trail[pl.ds(row, ROWS), columns(n)] = value.astype(jnp.bfloat16)

        fill(STRIPS - 1, 0, DETOUR * DETOURS)
        for k in range(DETOURS):
            d_copy(k, device(1, 0, s)).start()
        for n in range(STRIPS):
            fill(n, DETOUR * DETOURS if n == STRIPS - 1 else 0, states)
            b_copy(n).start()

    def take(i, row, count):
        x_copy(i, row, count).wait_recv()
        y_over(i, row, count, s).start()
        y_core(0, i, row, count, s).start()

    def relay(i, row, count):
        y_over(i, row, count, over).wait_recv()
        y_core(2, i, row, count, over).start()

    def have(i, row, count):
        view = left.at[pl.ds(0, 2), pl.ds(row, count)]
        same(view, y_send.at[0], c_recv.at[i % RING], device(p, h, core)).wait_recv()

    def stream(t):
        @pl.when(t < fine)
        def _():
            take(t, fine_row(t), FINE)

        @pl.when((t >= RELAY) & (t < fine + RELAY))
        def _():
            relay(t - RELAY, fine_row(t - RELAY), FINE)

    @pl.when((p == 1) & (h == 1))
    def _():
        loop(HAVE, stream)

    @pl.when((p == 1) & (h == 0))
    def _():
        for k in range(DETOURS):
            d_copy(k, device(0, 0, s)).wait_recv()
            d_copy(k, device(0, 0, s)).start()

    def near_stream(t):
        @pl.when(t < half)
        def _():
            take(t, half_rows(t, 1), ROWS)

        @pl.when((t >= NEAR_RELAY) & (t < half + NEAR_RELAY))
        def _():
            relay(t - NEAR_RELAY, half_rows(t - NEAR_RELAY, 1), ROWS)

    @pl.when((p == 0) & (h == 1))
    def _():
        loop(NEAR_FIRST, near_stream)

    @pl.when((p == 0) & (h == 0))
    def _():
        @functools.partial(loop, half)
        def _(i):
            relay(i, half_rows(i, 0), ROWS)

    same(infos.at[pl.ds(0, total - 1)], info_send.at[0], info_recv.at[0], device(p, h, core)).wait_recv()

    def emission(m, part):
        return infos[m * parts + part, :, 0:width]

    def peak(m):
        top = emission(m, 0)
        for part in range(1, parts):
            top = jnp.maximum(top, emission(m, part))
        return jnp.max(top, axis=1, keepdims=True)

    left_peak = jnp.where(p == 0, peak(0), peak(2))
    weights = [
        jnp.exp(jnp.where(p == 0, emission(0, part), emission(2, part)) - left_peak) for part in range(parts)
    ]
    middle_peak = peak(1)
    middle_emission = infos[parts + s, :, 0:width]
    middle_scale = jnp.exp(middle_emission - middle_peak) * 2.0 ** LEAD_SHIFT

    def product(row, count, n):
        acc = None
        for part in range(parts):
            lead = (left[part, pl.ds(row, count), :] * weights[part]).astype(jnp.bfloat16)
            block = slice(part * width, (part + 1) * width)
            right_block = trail[block, :] if n is None else trail[block, n * strip:(n + 1) * strip]
            term = jnp.dot(lead, right_block, preferred_element_type=jnp.float32)
            acc = term if acc is None else acc + term
        return acc

    @pl.when((p == 1) & (h == 1))
    def _():
        @functools.partial(loop, fine + HAVE, start=HAVE)
        def _(t):
            stream(t)

            i = t - HAVE
            row = fine_row(i)
            have(i, row, FINE)
            value = product(row, FINE, None) * 2.0 ** TRAIL_SHIFT
            pair[pl.ds(row, FINE), :] = value

            @pl.when(i >= fine - DIRECT)
            def _():
                pair_copy(2, i, device(0, 0, s)).start()

            pair_copy(0, i, device(0, 1, s)).start()
            pair_copy(1, i, device(1, 0, s)).start()
            paired[pl.ds(row, FINE), :] = value.astype(jnp.bfloat16)

            @pl.when((t >= fine - per_quarter) & (t < fine))
            def _():
                g = t - (fine - per_quarter)
                q_copy(g).wait_recv()
                g_core(0, g, s).start()
                v_copy(g).wait_recv()
                g_core(2, g, over).start()

    @pl.when((p == 0) & (h == 1))
    def _():
        @functools.partial(loop, half + NEAR_LATER, start=NEAR_FIRST)
        def _(t):
            near_stream(t)

            @pl.when((t >= NEAR_HAVE) & (t < half + NEAR_HAVE))
            def _():
                i = t - NEAR_HAVE
                g = i % per_quarter
                row = half_rows(i, 1)
                have(i, row, ROWS)
                value = product(row, ROWS, None) * middle_scale

                @pl.when(i < per_quarter)
                def _():
                    stage[pl.ds(local_row(g), ROWS), :] = value
                    w_copy(g).start()
                    q_copy(g).start()

                @pl.when(i >= per_quarter)
                def _():
                    first[s, pl.ds(local_row(g), ROWS), :] = value
                    g_over(g, s).start()
                    g_core(0, g, s).start()

            @pl.when(t >= NEAR_LATER)
            def _():
                i = t - NEAR_LATER
                g = i % per_quarter

                @pl.when(i < per_quarter)
                def _():
                    w_copy(g).wait_recv()
                    v_copy(g).start()

                @pl.when(i >= per_quarter)
                def _():
                    g_over(g, over).wait_recv()
                    g_core(2, g, over).start()

    unit = states // 16
    tile = quarter_rows // 4

    def partial_sum(row, ranges):
        acc = None
        for low, high in ranges:
            part, begin = low * unit // width, low * unit % width
            lead = first[part, pl.ds(row, tile), begin:begin + (high - low) * unit].astype(jnp.bfloat16)
            term = jnp.dot(lead, paired[low * unit:high * unit, :], preferred_element_type=jnp.float32)
            acc = term if acc is None else acc + term
        return acc

    def early_sum(i):
        row = pl.multiple_of(i * tile, tile)
        out_ref[pl.ds(row, tile), :] = partial_sum(row, EARLY)

    def middle_sum(i):
        row = pl.multiple_of(i * tile, tile)
        out_ref[pl.ds(row, tile), :] += partial_sum(row, MIDDLE)

    def wait_core(low, high, k):
        view = first.at[pl.ds(0, 2), :, pl.ds(low, high - low)]
        same(view, g_send.at[0], k_recv.at[k], device(p, h, core)).wait_recv()

    def strip_out(n, j):
        strip_over(n, j, s).start()
        strip_core(0, n, j, s).start()

    def strip_relay(n, j):
        strip_over(n, j, over).wait_recv()
        strip_core(2, n, j, over).start()

    def arrive(i):
        pair_copy(0, i, device(0, h, s)).wait_recv()

    def round_pair(i):
        row = fine_row(i)
        paired[pl.ds(row, FINE), :] = pair[pl.ds(row, FINE), :].astype(jnp.bfloat16)

    def relay_pair(i):
        arrive(i)

        @pl.when(i < fine - DIRECT)
        def _():
            pair_copy(0, i, device(0, 0, s)).start()

        round_pair(i)

    def strip_arrive(n, j):
        q_piece(n, j).wait_recv()
        strip_out(n, j)

    @pl.when((p == 1) & (h == 0))
    def _():
        for low, high, arrival, passing, part_row in SCHEDULE:
            loop(fine * high // 64, relay_pair, start=fine * low // 64)
            for j in range(PIECES):
                if arrival is not None:
                    strip_arrive(arrival, j)
                if passing is not None:
                    strip_relay(passing, j)
            if part_row == 0:
                wait_core(0, width - strip, 0)
            if part_row is not None:
                early_sum(part_row)
        done = 56
        for high, arrival, passing in LAST_SCHEDULE:
            loop(fine * high // 64, relay_pair, start=fine * done // 64)
            done = high
            if arrival is not None:
                strip_arrive(STRIPS - 1, arrival)
            if passing is not None:
                strip_relay(STRIPS - 1, passing)
        loop(fine * 63 // 64, relay_pair, start=fine * done // 64)

    @pl.when((p == 0) & (h == 0))
    def _():
        @functools.partial(loop, half)
        def _(i):
            have(i, half_rows(i, 0), ROWS)

        for n in range(STRIPS):
            b_copy(n).wait_recv()
            if n == STRIPS - 1:
                for k in range(DETOURS):
                    d_copy(k, device(1, 0, s)).wait_recv()

            @functools.partial(loop, chunks)
            def _(i):
                row = local_row(i)
                trail[pl.ds(row, ROWS), columns(n)] = right[pl.ds(row, ROWS), columns(n)].astype(jnp.bfloat16)

            scale = middle_scale[:, n * strip:(n + 1) * strip]
            for j in range(PIECES):
                stage[piece_rows(j), columns(n)] = product(2 * quarter_rows + j * piece, piece, n) * scale
                q_piece(n, j).start()
            for j in range(PIECES):
                first[s, piece_rows(j), columns(n)] = product(j * piece, piece, n) * scale
                strip_out(n, j)
            if n > 0:
                for j in range(PIECES):
                    strip_relay(n - 1, j)
        for j in range(PIECES):
            strip_relay(STRIPS - 1, j)

    first_cut = fine * 12 // 16
    second_cut = fine * 15 // 16

    def bring(low, high):
        def run(i, c):
            arrive(i)
            round_pair(i)
            return c
        lax.fori_loop(low, high, run, 0)

    @pl.when(p == 0)
    def _():
        bring(0, first_cut)

    @pl.when(h == 1)
    def _():
        wait_core(0, width, 0)
        loop(4, early_sum)

    @pl.when((h == 0) & (p == 0))
    def _():
        wait_core(0, width - strip, 0)
        loop(4, early_sum)

    @pl.when(h == 0)
    def _():
        wait_core(width - strip, width, 1)

    @pl.when(p == 0)
    def _():
        bring(first_cut, second_cut)

    loop(4, middle_sum)

    log_shares = jnp.zeros((1, 1), jnp.float32)
    for m in range(4):
        log_shares += infos[m * parts, :, width:width + 1]
    shift = math.log(2.0) * (LEAD_SHIFT + TRAIL_SHIFT)
    last_emission = jnp.zeros_like(middle_emission)
    for part in range(parts):
        last_emission = jnp.where(s == part, emission(3, part), last_emission)
    offset = last_emission + log_shares + (peak(0) + middle_peak + peak(2) - shift)

    offset_ref[...] = offset

    @pl.when(p == 0)
    def _():
        bring(second_cut, fine)

    @pl.when((p == 1) & (h == 0))
    def _():
        loop(fine, relay_pair, start=fine * 63 // 64)

    def store(i):
        rows = pl.ds(pl.multiple_of(i * tile, tile), tile)
        return pltpu.make_async_copy(out_ref.at[rows], out_hbm.at[rows], o_send.at[i])

    @functools.partial(loop, 4)
    def _(i):
        row = pl.multiple_of(i * tile, tile)
        out_ref[pl.ds(row, tile), :] += partial_sum(row, FINAL)
        store(i).start()

    same(infos.at[pl.ds(0, total - 1)], info_send.at[0], info_recv.at[0], device(p, h, core)).wait_send()

    def sent(view, sem):
        same(view, sem, load.at[0], device(p, h, core)).wait_send()

    def sent_left(count):
        for kind in range(3):
            sent(left.at[0, pl.ds(0, count)], y_send.at[kind])

    sent(first.at[0], g_send.at[0])
    sent(first.at[0], g_send.at[2])

    @pl.when((p == 0) | (h == 0))
    def _():
        sent(first.at[0], g_send.at[1])

    @pl.when((p == 1) & (h == 1))
    def _():
        sent_left(states)
        sent(pair, p_send.at[0])
        sent(pair, p_send.at[1])
        sent(pair.at[pl.ds(0, DIRECT * FINE)], p_send.at[2])

    @pl.when((p == 1) & (h == 0))
    def _():
        sent(left.at[0], x_send.at[0])
        sent(pair.at[pl.ds(0, states - DIRECT * FINE)], p_send.at[0])
        sent(right.at[pl.ds(0, DETOUR * DETOURS), columns(0)], d_send.at[0])

    @pl.when((p == 0) & (h == 1))
    def _():
        sent(right.at[pl.ds(0, states - DETOUR * DETOURS // STRIPS)], b_send.at[0])
        sent(right.at[pl.ds(0, DETOUR * DETOURS), columns(0)], d_send.at[0])
        sent_left(half_states)
        sent(stage.at[pl.ds(0, quarter_rows)], q_send.at[0])
        sent(stage.at[pl.ds(0, quarter_rows)], w_send.at[0])
        sent(stage.at[pl.ds(0, quarter_rows)], v_send.at[0])

    @pl.when((p == 0) & (h == 0))
    def _():
        sent(left.at[0, pl.ds(0, half_states)], x_send.at[0])
        sent_left(half_states)
        sent(stage.at[pl.ds(0, quarter_rows)], q_send.at[0])

    for i in range(4):
        store(i).wait()


def on_device(parts, trans_weight, pattern, boundary, log_emit):
    weight = trans_weight[0]
    states, width = weight.shape
    blocks = pattern.shape[0]
    packed = jnp.pad(pattern, ((0, 1), (0, width - blocks))).astype(jnp.float32) + jnp.pad(log_emit, ((blocks, 0), (0, 0)))
    fine = states // FINE
    groups = states // ROWS // 4
    dma = pltpu.SemaphoreType.DMA
    hbm = pl.BlockSpec(memory_space=pl.ANY)
    vmem = pl.BlockSpec(memory_space=pltpu.VMEM)
    total, offset = pl.pallas_call(
        functools.partial(kernel, parts),
        out_shape=(
            jax.ShapeDtypeStruct((states // 4, width), jnp.float32), jax.ShapeDtypeStruct((1, width), jnp.float32),
        ),
        in_specs=[hbm, vmem, pl.BlockSpec(memory_space=pltpu.SMEM)],
        out_specs=(hbm, vmem),
        scratch_shapes=[
            pltpu.VMEM((states // 4, width), jnp.float32),
            pltpu.VMEM((states, width), jnp.bfloat16),
            pltpu.VMEM((blocks, width), jnp.float32),
            pltpu.VMEM((1, width + BLOCK), jnp.float32),
            pltpu.VMEM((parts, states, width), jnp.float32),
            pltpu.VMEM((states, width), jnp.bfloat16),
            pltpu.VMEM((states, width), jnp.float32),
            pltpu.VMEM((states, width), jnp.bfloat16),
            pltpu.VMEM((parts, states // 4, width), jnp.float32),
            pltpu.VMEM((states // 2, width), jnp.float32),
            pltpu.VMEM((states, width), jnp.float32),
            pltpu.VMEM((4 * parts, 1, width + BLOCK), jnp.float32),
            dma((2,)), dma((1,)), dma((1,)),
            dma((1,)), dma((states // ROWS // 2,)),
            dma((3,)), dma((RING + max(2 * groups, STRIPS * PIECES),)), dma((RING,)),
            dma((3,)), dma((fine,)),
            dma((1,)), dma((3,)), dma((2,)),
            dma((1,)), dma((1,)), dma((1,)), dma((1,)), dma((4,)),
        ],
        compiler_params=pltpu.CompilerParams(
            collective_id=0, has_side_effects=True, vmem_limit_bytes=52 * 1024 * 1024
        ),
    )(weight, packed, boundary)
    return jnp.log(total) + offset


def solution(mesh):
    return jax.shard_map(
        functools.partial(on_device, mesh.shape["state"]),
        mesh=mesh,
        in_specs=(P("tm", None, "state"), P(), P("tm"), P("tm", "state")),
        out_specs=P("tm", "state"),
        check_vma=False,
    )
```
